32 devices in a mesh: fsdp: 8 (over z, y), seq: 4 (over x, core).
Axes of the slice: x: 2, y: 2, z: 4, core: 2. Of those that a mesh axis runs over, the one named last changes fastest.
Arguments:
- inputs: bfloat16 [16, 1024, 768], P('fsdp', 'seq'), may hold values from -6 to 6
- segments: int32 [16, 1024], P('fsdp'), may hold values from 0 to 7, never falling along the last dimension, each value on 1 to 512 neighbouring positions
- neighbours: bfloat16 [16, 16, 256, 768], P('fsdp', 'seq'), may hold values from -6 to 6
- ln1_gain: bfloat16 [768], P('fsdp'), may hold values from 0.5 to 1.5
- ln1_bias: bfloat16 [768], P('fsdp'), may hold values from -3 to 3
- w_qkv: bfloat16 [768, 2304], P('fsdp'), may hold values from -0.21875 to 0.21875
- w_attn_out: bfloat16 [768, 768], P('fsdp'), may hold values from -0.875 to 0.875
- ln2_gain: bfloat16 [768], P('fsdp'), may hold values from 0.5 to 1.5
- ln2_bias: bfloat16 [768], P('fsdp'), may hold values from -3 to 3
- cross_q: bfloat16 [768, 768], P('fsdp'), may hold values from -0.21875 to 0.21875
- cross_kv: bfloat16 [768, 1536], P('fsdp'), may hold values from -0.21875 to 0.21875
- cross_out: bfloat16 [768, 768], P('fsdp'), may hold values from -1.25 to 1.25
- ln3_gain: bfloat16 [768], P('fsdp'), may hold values from 0.5 to 1.5
- ln3_bias: bfloat16 [768], P('fsdp'), may hold values from -3 to 3
- w_up: bfloat16 [768, 3072], P('fsdp'), may hold values from -0.21875 to 0.21875
- w_down: bfloat16 [3072, 768], P('fsdp'), may hold values from -0.109375 to 0.109375
- out_grad: bfloat16 [16, 1024, 768], P('fsdp', 'seq'), may hold values from -6 to 6
Outputs:
- outputs: bfloat16 [16, 1024, 768], P('fsdp', 'seq')
- input_grad: float32 [16, 1024, 768], P('fsdp', 'seq')
- neighbour_grad: float32 [16, 16, 256, 768], P('fsdp', 'seq')
- grad_ln1_gain: float32 [768], P('fsdp')
- grad_ln1_bias: float32 [768], P('fsdp')
- grad_w_qkv: float32 [768, 2304], P('fsdp')
- grad_w_attn_out: float32 [768, 768], P('fsdp')
- grad_ln2_gain: float32 [768], P('fsdp')
- grad_ln2_bias: float32 [768], P('fsdp')
- grad_cross_q: float32 [768, 768], P('fsdp')
- grad_cross_kv: float32 [768, 1536], P('fsdp')
- grad_cross_out: float32 [768, 768], P('fsdp')
- grad_ln3_gain: float32 [768], P('fsdp')
- grad_ln3_bias: float32 [768], P('fsdp')
- grad_w_up: float32 [768, 3072], P('fsdp')
- grad_w_down: float32 [3072, 768], P('fsdp')
The draws below stay inside these ranges and needn't reach their ends.
Inputs may be any that keep to these rules, and one draw needn't show every extreme that they name: `segments`: along each sequence the segment numbers never fall; each of its 8 documents has 1 to 512 tokens, and one has exactly 512.
All inputs are finite; a program needn't handle non-finite values.
Results may differ from the reference program's by a relative error of at most 0.02.
Values may be sent and summed in bfloat16 or wider, within the bound.
No kernel may reach another device: no remote copies, remote signals or barrier semaphores. Data moves between devices by JAX's collectives and lax.ppermute only.
A program may use at most 192 MiB of HBM per device.

```python
import math
import jax
import jax.numpy as jnp
import numpy as np
from jax import lax

D = 768
HEADS = 12
HEAD_DIM = 64
FF = 3072
SPAN = 64
LENGTH = 1024
DOCS = 8
NTOK = 256
SPANS = 16
SEQS = 16


def level_of(stream_key, dims, pieces, least, top_value):
    def one(axis_at, parts):
        heights = jax.random.uniform(jax.random.fold_in(jax.random.fold_in(stream_key, 6), axis_at), (parts,), jnp.float32, least / len(pieces), top_value / len(pieces))
        return jnp.repeat(jnp.exp(heights), dims[axis_at] // parts).reshape((-1,) + (1,) * (len(dims) - axis_at - 1))

    level = one(*pieces[0])
    for cut in pieces[1:]:
        level = level * one(*cut)
    return level


def split_up(amount, total, reach, lean):
    weights = [(1 << 20) // math.isqrt(rank ** lean) + 1 for rank in range(2, amount + 1)]
    rest, counts = total - reach - (amount - 1), [1] * (amount - 1)
    while rest > 0:
        candidates = [i for i in range(amount - 1) if counts[i] < reach]
        pool, budget = sum([weights[i] for i in candidates]), rest
        for i in candidates:
            addition = min(reach - counts[i], max(1, budget * weights[i] // pool), rest)
            counts[i] = counts[i] + addition
            rest = rest - addition
    return np.array([reach] + counts)


def uneven_parts(key, number_of, total, most, skew):
    if number_of == 2:
        one = jax.random.randint(key, (), max(1, total - most), min(most, total - 1) + 1)
        return jnp.stack([one, total - one])
    sizes = jnp.asarray(split_up(number_of, total, most, skew), jnp.int32)
    couples = (number_of - 1) // 2
    giver, receiver = sizes[1:1 + 2 * couples:2], sizes[2:2 + 2 * couples:2]
    margin = jnp.minimum(giver - 1, most - receiver)
    moved = jax.random.randint(jax.random.fold_in(key, 1), (couples,), 0, 1 << 20) % (margin + 1)
    sizes = sizes.at[1:1 + 2 * couples:2].set(giver - moved).at[2:2 + 2 * couples:2].set(receiver + moved)
    return sizes[jax.random.permutation(jax.random.fold_in(key, 2), number_of)]


def noise(rng, dims, scale, reach, split=(), dtype=jnp.bfloat16):
    array = scale * jax.random.normal(rng, dims, jnp.float32)
    if split:
        array = array * level_of(rng, dims, split, -0.22, 0.18)
    return jnp.clip(array, -reach, reach).astype(dtype)


def setup_inputs(seed: int = 0) -> dict:
    key_list = jax.random.split(jax.random.key(seed), 18)
    return {
        "inputs": noise(key_list[0], (SEQS, LENGTH, D), 1.0, 6.0, ((0, 8), (1, 4))),
        "segments": jax.vmap(lambda own: jnp.searchsorted(jnp.cumsum(uneven_parts(own, DOCS, LENGTH, LENGTH // 2, 2)), jnp.arange(LENGTH), side="right"))(jax.random.split(key_list[1], SEQS)).reshape((SEQS, LENGTH)).astype(jnp.int32),
        "neighbours": noise(key_list[2], (SEQS, SPANS, NTOK, D), 1.0, 6.0, ((0, 8), (1, 4))),
        "ln1_gain": jnp.clip(1.0 + 0.1 * jax.random.normal(key_list[3], (D,), jnp.float32), 0.5, 1.5).astype(jnp.bfloat16),
        "ln1_bias": noise(key_list[4], (D,), 0.5, 3.0, ((0, 8),)),
        "w_qkv": noise(key_list[5], (D, 3 * D), D ** -0.5, 0.21875, ((0, 8),)),
        "w_attn_out": noise(key_list[6], (D, D), (D // 16) ** -0.5, 0.875, ((0, 8),)),
        "ln2_gain": jnp.clip(1.0 + 0.1 * jax.random.normal(key_list[7], (D,), jnp.float32), 0.5, 1.5).astype(jnp.bfloat16),
        "ln2_bias": noise(key_list[8], (D,), 0.5, 3.0, ((0, 8),)),
        "cross_q": noise(key_list[9], (D, D), D ** -0.5, 0.21875, ((0, 8),)),
        "cross_kv": noise(key_list[10], (D, 2 * D), D ** -0.5, 0.21875, ((0, 8),)),
        "cross_out": noise(key_list[11], (D, D), (D // 32) ** -0.5, 1.25, ((0, 8),)),
        "ln3_gain": jnp.clip(1.0 + 0.1 * jax.random.normal(key_list[12], (D,), jnp.float32), 0.5, 1.5).astype(jnp.bfloat16),
        "ln3_bias": noise(key_list[13], (D,), 0.5, 3.0, ((0, 8),)),
        "w_up": noise(key_list[14], (D, FF), D ** -0.5, 0.21875, ((0, 8),)),
        "w_down": noise(key_list[15], (FF, D), FF ** -0.5, 0.109375, ((0, 8),)),
        "out_grad": noise(key_list[16], (SEQS, LENGTH, D), 1.0, 6.0, ((0, 8), (1, 4))),
    }


EPS = 1e-05
NEG = -1e+30
HIGH = lax.Precision.HIGHEST

@jax.custom_vjp
def low(v):
    return lax.optimization_barrier(v.astype(jnp.bfloat16)).astype(jnp.float32)

@jax.custom_vjp
def low_back(v):
    return v

def low_keep(v):
    return (low(v), None)

def low_pass(kept, grad):
    return (grad,)

def back_keep(v):
    return (v, None)

def back_low(kept, grad):
    return (low(grad),)
low.defvjp(low_keep, low_pass)
low_back.defvjp(back_keep, back_low)

def layer_norm(values, gain_row, bias_row):
    centre = values - lax.optimization_barrier(jnp.mean(values, -1, keepdims=True))
    spread = lax.optimization_barrier(jnp.mean(centre * centre, -1, keepdims=True))
    return centre * lax.rsqrt(spread + EPS) * gain_row + bias_row

def gelu_tanh(values):
    return jax.nn.gelu(values, approximate=True)

def soft_weights(scores):
    row_top = lax.optimization_barrier(jnp.max(scores, -1, keepdims=True))
    raised = jnp.exp(scores - row_top)
    return raised / lax.optimization_barrier(jnp.sum(raised, -1, keepdims=True))

def matmul_high(left_side, right_side):
    return jnp.dot(left_side, right_side, precision=HIGH)

def forward(params, tokens, seg_row, neighbour_rows):
    gain_one, bias_one, w_qkv, w_attn_out, gain_two, bias_two, cross_q, cross_kv, cross_out, gain_three, bias_three, w_up, w_down = params
    length = tokens.shape[0]
    score_scale = HEAD_DIM ** (-0.5)
    normed = low(layer_norm(tokens, gain_one, bias_one))
    packed = low(low_back(matmul_high(normed, w_qkv))).reshape(length, 3, HEADS, HEAD_DIM)
    scores = low_back(jnp.einsum('qhd,khd->hqk', packed[:, 0], packed[:, 1], precision=HIGH) * score_scale)
    places = jnp.arange(length)
    allowed = (seg_row[:, None] == seg_row[None, :]) & (places[None, :] <= places[:, None])
    weights = low(soft_weights(jnp.where(allowed[None], scores, NEG)))
    mixed_heads = jnp.einsum('hqk,khd->qhd', weights, packed[:, 2], precision=HIGH).reshape(length, D)
    mixed_heads = low(low_back(mixed_heads))
    after_self = tokens + low_back(matmul_high(mixed_heads, w_attn_out))
    normed_two = low(layer_norm(after_self, gain_two, bias_two))
    spans = length // SPAN
    query_spans = low(low_back(matmul_high(normed_two, cross_q))).reshape(spans, SPAN, HEADS, HEAD_DIM)
    memory = low(low_back(matmul_high(neighbour_rows.reshape(spans * NTOK, D), cross_kv)))
    memory = memory.reshape(spans, NTOK, 2, HEADS, HEAD_DIM)
    cross_scores = low_back(jnp.einsum('cqhd,ckhd->chqk', query_spans, memory[:, :, 0], precision=HIGH) * score_scale)
    cross_weights = low(soft_weights(cross_scores))
    cross_mixed = jnp.einsum('chqk,ckhd->cqhd', cross_weights, memory[:, :, 1], precision=HIGH).reshape(length, D)
    cross_mixed = low(low_back(cross_mixed))
    after_cross = after_self + low_back(matmul_high(cross_mixed, cross_out))
    normed_three = low(layer_norm(after_cross, gain_three, bias_three))
    hidden = low_back(matmul_high(normed_three, w_up))
    activated = low(gelu_tanh(hidden))
    return after_cross + low_back(matmul_high(activated, w_down))

def reference(inputs, segments, neighbours, ln1_gain, ln1_bias, w_qkv, w_attn_out, ln2_gain, ln2_bias, cross_q, cross_kv, cross_out, ln3_gain, ln3_bias, w_up, w_down, out_grad):
    params = tuple((array_in.astype(jnp.float32) for array_in in (ln1_gain, ln1_bias, w_qkv, w_attn_out, ln2_gain, ln2_bias, cross_q, cross_kv, cross_out, ln3_gain, ln3_bias, w_up, w_down)))

    def per_sequence(running, sliced):
        tokens, seg_row, neighbour_rows, cotangent = sliced

        def apply_layer(param_set, token_rows, memory_rows):
            return forward(param_set, token_rows, seg_row, memory_rows)
        result, pull_back = jax.vjp(apply_layer, params, tokens.astype(jnp.float32), neighbour_rows.astype(jnp.float32))
        param_grads, token_grads, memory_grads = pull_back(cotangent.astype(jnp.float32))
        running = tuple((running_sum + grad_part for running_sum, grad_part in zip(running, param_grads)))
        return (running, (result.astype(jnp.bfloat16), token_grads, memory_grads))
    start_sums = tuple((jnp.zeros(array_in.shape, jnp.float32) for array_in in params))
    grad_sums, (outputs, input_grad, neighbour_grad) = lax.scan(per_sequence, start_sums, (inputs, segments, neighbours, out_grad))
    return (outputs, input_grad, neighbour_grad, grad_sums[0], grad_sums[1], grad_sums[2], grad_sums[3], grad_sums[4], grad_sums[5], grad_sums[6], grad_sums[7], grad_sums[8], grad_sums[9], grad_sums[10], grad_sums[11], grad_sums[12])
```

```python
import functools

import jax
import jax.numpy as jnp
from jax import lax
from jax.experimental import pallas as pl
from jax.experimental.pallas import tpu as pltpu
from jax.sharding import PartitionSpec as P

HEADS = 12
HEAD_DIM = 64
SPAN = 64
EPS = 1e-05
NEG = -1e30
WINDOW = 512
SCALE = HEAD_DIM ** (-0.5)
BF = jnp.bfloat16
F32 = jnp.float32
LIMIT = 60 * 1024 * 1024

GELU_A = 0.7978845608028654
GELU_B = 0.044715


def dot(a, b):
    return lax.dot_general(a, b, (((1,), (0,)), ((), ())), preferred_element_type=F32)


def dot_nt(a, b):
    return lax.dot_general(a, b, (((1,), (1,)), ((), ())), preferred_element_type=F32)


def dot_tn(a, b):
    return lax.dot_general(a, b, (((0,), (0,)), ((), ())), preferred_element_type=F32)


def params(**kw):
    return pltpu.CompilerParams(vmem_limit_bytes=LIMIT, **kw)


def head_mask(rows, head):
    lane = lax.broadcasted_iota(jnp.int32, (rows, 2 * HEAD_DIM), 1)
    return (lane < HEAD_DIM) if head == 0 else (lane >= HEAD_DIM)


def allowed_keys(segc_ref, segr_ref, k0, k1, q0, q1):
    same = segc_ref[k0:k1, :] == segr_ref[:, q0:q1]
    kpos = lax.broadcasted_iota(jnp.int32, (k1 - k0, q1 - q0), 0) + k0
    qpos = lax.broadcasted_iota(jnp.int32, (k1 - k0, q1 - q0), 1) + q0
    return same & (kpos <= qpos)


def self_fwd_kernel(q_ref, k_ref, v_ref, segc_ref, segr_ref, o_ref, lse_ref, vt_ref, *, block):
    length = q_ref.shape[0]
    vt_ref[...] = v_ref[...].astype(F32).T.astype(BF)
    row = lax.broadcasted_iota(jnp.int32, (2 * HEAD_DIM, block), 0)
    for q0 in range(0, length, block):
        q1 = q0 + block
        k0 = max(0, q0 - WINDOW)
        keep = allowed_keys(segc_ref, segr_ref, k0, q1, q0, q1)
        q = q_ref[q0:q1, :]
        outs = []
        for head in range(2):
            qh = jnp.where(head_mask(block, head), q * SCALE, 0).astype(BF)
            s = jnp.where(keep, dot_nt(k_ref[k0:q1, :], qh), NEG)
            top = jnp.max(s, 0, keepdims=True)
            e = jnp.exp(s - top)
            total = jnp.sum(e, 0, keepdims=True)
            outs.append(dot(vt_ref[:, k0:q1], e.astype(BF)) / total)
            lse_ref[0, head : head + 1, q0:q1] = top + jnp.log(total)
        o = jnp.where(row < HEAD_DIM, outs[0], outs[1])
        o_ref[q0:q1, :] = o.T.astype(BF)


def self_forward(qkv, segc, segr):
    length, width = qkv.shape
    pairs = width // (6 * HEAD_DIM)
    pair = 2 * HEAD_DIM
    return pl.pallas_call(
        functools.partial(self_fwd_kernel, block=256),
        grid=(pairs,),
        in_specs=[
            pl.BlockSpec((length, pair), lambda j: (0, j)),
            pl.BlockSpec((length, pair), lambda j: (0, pairs + j)),
            pl.BlockSpec((length, pair), lambda j: (0, 2 * pairs + j)),
            pl.BlockSpec((length, 1), lambda j: (0, 0)),
            pl.BlockSpec((1, length), lambda j: (0, 0)),
        ],
        out_specs=[
            pl.BlockSpec((length, pair), lambda j: (0, j)),
            pl.BlockSpec((1, 8, length), lambda j: (j, 0, 0)),
        ],
        out_shape=[
            jax.ShapeDtypeStruct((length, pairs * pair), BF),
            jax.ShapeDtypeStruct((pairs, 8, length), F32),
        ],
        scratch_shapes=[pltpu.VMEM((pair, length), BF)],
        compiler_params=params(),
        cost_estimate=pl.CostEstimate(
            flops=8 * pairs * length * length * HEAD_DIM,
            bytes_accessed=10 * length * pairs * pair,
            transcendentals=2 * pairs * length * length // 2,
        ),
        name="self_forward",
    )(qkv, qkv, qkv, segc, segr)


def self_bwd_kernel(
    q_ref, k_ref, v_ref, do_ref, segc_ref, segr_ref, lse_ref, dq_ref, dk_ref, dv_ref, kt_ref, dka, dva, *, block
):
    length = q_ref.shape[0]
    kt_ref[...] = k_ref[...].astype(F32).T.astype(BF)
    dka[...] = jnp.zeros_like(dka)
    dva[...] = jnp.zeros_like(dva)
    row = lax.broadcasted_iota(jnp.int32, (2 * HEAD_DIM, block), 0)
    for q0 in range(0, length, block):
        q1 = q0 + block
        k0 = max(0, q0 - WINDOW)
        keep = allowed_keys(segc_ref, segr_ref, k0, q1, q0, q1)
        q = q_ref[q0:q1, :]
        do = do_ref[q0:q1, :]
        dqs = []
        for head in range(2):
            mine = head_mask(block, head)
            qh = jnp.where(mine, q * SCALE, 0).astype(BF)
            doh = jnp.where(mine, do, 0).astype(BF)
            s = jnp.where(keep, dot_nt(k_ref[k0:q1, :], qh), NEG)
            p = jnp.exp(s - lse_ref[0, head : head + 1, q0:q1])
            dp = dot_nt(v_ref[k0:q1, :], doh)
            delta = jnp.sum(p * dp, 0, keepdims=True)
            ds = (p * (dp - delta)).astype(BF)
            dka[k0:q1, :] += dot(ds, qh)
            dva[k0:q1, :] += dot(p.astype(BF), doh)
            dqs.append(dot(kt_ref[:, k0:q1], ds))
        dq = jnp.where(row < HEAD_DIM, dqs[0], dqs[1]) * SCALE
        dq_ref[q0:q1, :] = dq.T.astype(BF)
    dk_ref[...] = dka[...].astype(BF)
    dv_ref[...] = dva[...].astype(BF)


def self_backward(qkv, do, segc, segr, lse):
    length, width = qkv.shape
    pairs = width // (6 * HEAD_DIM)
    pair = 2 * HEAD_DIM
    column = pl.BlockSpec((length, pair), lambda j: (0, j))
    return pl.pallas_call(
        functools.partial(self_bwd_kernel, block=256),
        grid=(pairs,),
        in_specs=[
            column,
            pl.BlockSpec((length, pair), lambda j: (0, pairs + j)),
            pl.BlockSpec((length, pair), lambda j: (0, 2 * pairs + j)),
            column,
            pl.BlockSpec((length, 1), lambda j: (0, 0)),
            pl.BlockSpec((1, length), lambda j: (0, 0)),
            pl.BlockSpec((1, 8, length), lambda j: (j, 0, 0)),
        ],
        out_specs=[column] * 3,
        out_shape=[jax.ShapeDtypeStruct((length, pairs * pair), BF)] * 3,
        scratch_shapes=[
            pltpu.VMEM((pair, length), BF),
            pltpu.VMEM((length, pair), F32),
            pltpu.VMEM((length, pair), F32),
        ],
        compiler_params=params(),
        cost_estimate=pl.CostEstimate(
            flops=20 * pairs * length * length * HEAD_DIM,
            bytes_accessed=16 * length * pairs * pair,
            transcendentals=pairs * length * length,
        ),
        name="self_backward",
    )(qkv, qkv, qkv, do, segc, segr, lse)


def stack_heads(block):
    rows = block.shape[0]
    return jnp.concatenate(
        [jnp.where(head_mask(rows, head), block, 0) for head in range(2)], 0
    ).astype(BF)


def unstack_heads(block):
    rows = block.shape[0] // 2
    return jnp.where(head_mask(rows, 0), block[:rows], block[rows:])


def cross_weights(k, qs):
    s = dot_nt(k, qs)
    e = jnp.exp(s - jnp.max(s, 0, keepdims=True))
    return e, jnp.sum(e, 0, keepdims=True)


def cross_fwd_kernel(q_ref, k_ref, v_ref, o_ref):
    pair = 2 * HEAD_DIM
    for at in range(0, q_ref.shape[1], pair):
        cols = slice(at, at + pair)
        qs = stack_heads(q_ref[:, cols] * SCALE)
        e, total = cross_weights(k_ref[:, cols], qs)
        o = dot_tn((e / total).astype(BF), v_ref[:, cols])
        o_ref[:, cols] = unstack_heads(o).astype(BF)


def cross_forward(cq, ckv):
    tokens, width = cq.shape
    spans = tokens // SPAN
    memory = ckv.shape[0] // spans
    return pl.pallas_call(
        cross_fwd_kernel,
        grid=(spans,),
        in_specs=[
            pl.BlockSpec((SPAN, width), lambda i: (i, 0)),
            pl.BlockSpec((memory, width), lambda i: (i, 0)),
            pl.BlockSpec((memory, width), lambda i: (i, 1)),
        ],
        out_specs=pl.BlockSpec((SPAN, width), lambda i: (i, 0)),
        out_shape=jax.ShapeDtypeStruct((tokens, width), BF),
        compiler_params=params(),
        cost_estimate=pl.CostEstimate(
            flops=4 * tokens * memory * width,
            bytes_accessed=4 * tokens * width + 4 * spans * memory * width,
            transcendentals=tokens * memory * HEADS,
        ),
        name="cross_forward",
    )(cq, ckv, ckv)


def cross_bwd_kernel(q_ref, k_ref, v_ref, do_ref, dq_ref, dkv_ref):
    pair = 2 * HEAD_DIM
    width = q_ref.shape[1]
    for at in range(0, width, pair):
        cols = slice(at, at + pair)
        qs = stack_heads(q_ref[:, cols] * SCALE)
        dos = stack_heads(do_ref[:, cols])
        k = k_ref[:, cols]
        e, total = cross_weights(k, qs)
        p = e / total
        dp = dot_nt(v_ref[:, cols], dos)
        delta = jnp.sum(p * dp, 0, keepdims=True)
        ds = (p * (dp - delta)).astype(BF)
        dq_ref[:, cols] = (unstack_heads(dot_tn(ds, k)) * SCALE).astype(BF)
        dkv_ref[:, cols] = dot(ds, qs).astype(BF)
        dkv_ref[:, width + at : width + at + pair] = dot(p.astype(BF), dos).astype(BF)


def cross_backward(cq, ckv, do):
    tokens, width = cq.shape
    spans = tokens // SPAN
    memory = ckv.shape[0] // spans
    return pl.pallas_call(
        cross_bwd_kernel,
        grid=(spans,),
        in_specs=[
            pl.BlockSpec((SPAN, width), lambda i: (i, 0)),
            pl.BlockSpec((memory, width), lambda i: (i, 0)),
            pl.BlockSpec((memory, width), lambda i: (i, 1)),
            pl.BlockSpec((SPAN, width), lambda i: (i, 0)),
        ],
        out_specs=[
            pl.BlockSpec((SPAN, width), lambda i: (i, 0)),
            pl.BlockSpec((memory, 2 * width), lambda i: (i, 0)),
        ],
        out_shape=[
            jax.ShapeDtypeStruct((tokens, width), BF),
            jax.ShapeDtypeStruct((spans * memory, 2 * width), BF),
        ],
        compiler_params=params(),
        cost_estimate=pl.CostEstimate(
            flops=10 * tokens * memory * width,
            bytes_accessed=6 * tokens * width + 8 * spans * memory * width,
            transcendentals=tokens * memory * HEADS,
        ),
        name="cross_backward",
    )(cq, ckv, ckv, do)


def ffn_kernel(h_ref, dy_ref, *refs, quarters, carry, chunk):
    ups, downs = refs[:quarters], refs[quarters : 2 * quarters]
    rest = refs[2 * quarters :]
    if carry:
        y0_ref, dh0_ref, rest = rest[0], rest[1], rest[2:]
    y_ref, dh_ref = rest[0], rest[1]
    grads = rest[2:]
    step = pl.program_id(0)
    width = h_ref.shape[1]

    @pl.when(step == 0)
    def _():
        y_ref[...] = y0_ref[...] if carry else jnp.zeros_like(y_ref)
        dh_ref[...] = dh0_ref[...] if carry else jnp.zeros_like(dh_ref)

    h = h_ref[...]
    dy = dy_ref[...]
    at = pl.multiple_of(step * chunk, chunk)
    for up_ref, down_ref, g_ref in zip(ups, downs, grads):
        up, down = up_ref[...], down_ref[...]
        u = dot(h, up)
        t = jnp.tanh(GELU_A * (u + GELU_B * (u * u * u)))
        gl = (0.5 * u * (1.0 + t)).astype(BF)
        y_ref[...] += dot(gl, down)
        slope = 0.5 * (1.0 + t) + 0.5 * u * (1.0 - t * t) * (GELU_A * (1.0 + 3.0 * GELU_B * (u * u)))
        du = (dot_nt(dy, down) * slope).astype(BF)
        dh_ref[...] += dot_nt(du, up)
        g_ref[:, pl.ds(at, chunk)] = dot_tn(h, du).astype(BF)
        g_ref[pl.ds(at, chunk), pl.ds(width, width)] = dot_tn(gl, dy).astype(BF)


def feed_forward(h, dy, weights, carry=None):
    tokens, width = h.shape
    n = len(weights)
    hidden = weights[0].shape[0]
    chunk = 256
    whole = pl.BlockSpec((tokens, width), lambda j: (0, 0))
    operands = [h, dy, *weights, *weights]
    in_specs = [whole, whole]
    in_specs += [pl.BlockSpec((width, chunk), lambda j: (0, j))] * n
    in_specs += [pl.BlockSpec((chunk, width), lambda j: (j, 1))] * n
    if carry is not None:
        operands += list(carry)
        in_specs += [whole, whole]
    out = pl.pallas_call(
        functools.partial(ffn_kernel, quarters=n, carry=carry is not None, chunk=chunk),
        grid=(hidden // chunk,),
        in_specs=in_specs,
        out_specs=[whole, whole] + [pl.BlockSpec((hidden, 2 * width), lambda j: (0, 0))] * n,
        out_shape=[jax.ShapeDtypeStruct((tokens, width), F32)] * 2
        + [jax.ShapeDtypeStruct((hidden, 2 * width), BF)] * n,
        compiler_params=params(),
        cost_estimate=pl.CostEstimate(
            flops=12 * n * tokens * width * hidden,
            bytes_accessed=8 * n * width * hidden + 16 * tokens * width,
            transcendentals=n * tokens * hidden,
        ),
        name="feed_forward",
    )(*operands)
    return out[0], out[1], out[2:]


def assemble_kernel(idx_ref, *refs, n, rows):
    pieces, out_ref, sem = refs[:n], refs[n], refs[n + 1]
    copies = []
    for i in range(n):
        at = pl.multiple_of(idx_ref[i] * rows, rows)
        copies.append(pltpu.make_async_copy(pieces[i], out_ref.at[pl.ds(at, rows), :], sem.at[i]))
    for copy in copies:
        copy.start()
    for copy in copies:
        copy.wait()


def assemble(pieces, places):
    rows, cols = pieces[0].shape
    n = len(pieces)
    return pl.pallas_call(
        functools.partial(assemble_kernel, n=n, rows=rows),
        grid_spec=pltpu.PrefetchScalarGridSpec(
            num_scalar_prefetch=1,
            grid=(1,),
            in_specs=[pl.BlockSpec(memory_space=pl.ANY)] * n,
            out_specs=pl.BlockSpec((n * rows, cols), lambda i, idx: (0, 0)),
            scratch_shapes=[pltpu.SemaphoreType.DMA((n,))],
        ),
        out_shape=jax.ShapeDtypeStruct((n * rows, cols), pieces[0].dtype),
        compiler_params=params(),
        cost_estimate=pl.CostEstimate(
            flops=0, bytes_accessed=4 * n * rows * cols, transcendentals=0
        ),
        name="assemble",
    )(jnp.stack(places).astype(jnp.int32), *pieces)


class Place:
    def __init__(self):
        self.n = lax.axis_size("fsdp")
        f = lax.axis_index("fsdp")
        s = lax.axis_index("seq")
        self.z, self.y = f // 2, f % 2
        self.x, self.c = s // 2, s % 2
        self.s = s
        self.direct = self.n == 8

    def swap_core(self, value):
        return lax.ppermute(value, "seq", [(0, 1), (1, 0), (2, 3), (3, 2)])

    def swap_x(self, value):
        return lax.ppermute(value, "seq", [(0, 2), (2, 0), (1, 3), (3, 1)])

    def swap_y(self, value):
        return lax.ppermute(value, "fsdp", [(i, i ^ 1) for i in range(self.n)])

    def shift_z(self, value, hops):
        return lax.ppermute(value, "fsdp", [(i, (i + 2 * hops) % self.n) for i in range(self.n)])

    def gather(self, piece):
        if not self.direct:
            return lax.all_gather(piece, "fsdp", axis=0, tiled=True)
        columns = [piece] + [self.shift_z(piece, k) for k in (1, 2, 3)]
        others = [self.swap_y(p) for p in columns]
        base = [2 * ((self.z - k) % 4) for k in range(4)]
        return assemble(
            columns + others, [b + self.y for b in base] + [b + 1 - self.y for b in base]
        )

    def scatter(self, blocks):
        rows, cols = blocks.shape[1:]
        if not self.direct:
            return lax.psum_scatter(
                blocks.astype(BF), "fsdp", scatter_dimension=0, tiled=False
            ).astype(F32)
        blocks = blocks.reshape(4, 2, rows, cols)
        sent = pick(blocks, 1 - self.y, 1)
        kept = pick(blocks, self.y, 1)
        column = (kept.astype(F32) + self.swap_y(sent.astype(BF)).astype(F32)).astype(BF)
        total = pick(column, self.z, 0).astype(F32)
        for k in (1, 2, 3):
            total = total + self.shift_z(pick(column, (self.z + k) % 4, 0), k).astype(F32)
        return total


def pick(value, index, axis):
    return lax.dynamic_index_in_dim(value, index, axis, keepdims=False)


def ordered(flag, first, second, axis):
    low = jnp.where(flag == 0, first, second)
    high = jnp.where(flag == 0, second, first)
    return jnp.stack([low, high], axis)


def norm_stats(values):
    centre = values - jnp.mean(values, -1, keepdims=True)
    r = lax.rsqrt(jnp.mean(centre * centre, -1, keepdims=True) + EPS)
    return centre * r, r


def norm(values, gain, bias):
    xhat, _ = norm_stats(values)
    return (xhat * gain + bias).astype(BF)


def norm_back(values, gain, dh):
    xhat, r = norm_stats(values)
    dg = dh * gain
    dv = r * (
        dg - jnp.mean(dg, -1, keepdims=True) - xhat * jnp.mean(dg * xhat, -1, keepdims=True)
    )
    return dv, jnp.sum(dh * xhat, 0), jnp.sum(dh, 0)


def per_device(
    inputs, segments, neighbours,
    ln1_gain, ln1_bias, w_qkv, w_attn_out, ln2_gain, ln2_bias, cross_q, cross_kv, cross_out,
    ln3_gain, ln3_bias, w_up, w_down, out_grad,
):
    at = Place()
    x, c = at.x, at.c
    seqs, piece, width = inputs.shape
    half = width // 2
    rows = w_qkv.shape[0]
    tokens = seqs * piece

    theirs = at.swap_x(pick(inputs, 1 - x, 0))
    mine = pick(inputs, x, 0)
    blocks = ordered(x, mine, theirs, 0)
    sequence = ordered(c, blocks, at.swap_core(blocks), 1).reshape(4 * piece, width)
    seg = pick(segments, x, 0)
    segc, segr = seg[:, None], seg[None, :]

    vectors = jnp.stack([ln1_gain, ln1_bias, ln2_gain, ln2_bias, ln3_gain, ln3_bias], 1)
    vectors = jnp.pad(vectors, ((0, 0), (0, 128 - vectors.shape[1])))
    qkv_half = pick(w_qkv.reshape(rows, 3, 2, half), c, 2).reshape(rows, 3 * half)
    group_a = at.gather(jnp.concatenate([qkv_half, vectors], 1))
    wqkv = group_a[:, : 3 * half]
    gains = group_a[:, 3 * half : 3 * half + 6].T.astype(F32)
    g1, b1, g2, b2, g3, b3 = (gains[i] for i in range(6))

    def half_of(weight):
        return lax.dynamic_slice_in_dim(weight, c * (weight.shape[1] // 2), weight.shape[1] // 2, 1)

    group_b = at.gather(
        jnp.concatenate([half_of(w) for w in (cross_kv, w_attn_out, cross_q, cross_out)], 1)
    )
    group_b2 = at.swap_core(group_b)

    def both(start, size):
        a, b = group_b[:, start : start + size], group_b2[:, start : start + size]
        return ordered(c, a, b, 1).reshape(width, 2 * size)

    wckv = both(0, width)
    wao = both(width, half)
    wcq = both(width + half, half)
    wco = both(2 * width, half)

    unit = w_down.shape[0] // 4
    up_quarter = pick(w_up.reshape(rows, -1, 4, unit), at.s, 2).reshape(rows, -1)
    down_quarter = pick(w_down.reshape(4, unit, width), at.s, 0)
    q00 = at.gather(jnp.concatenate([up_quarter, down_quarter], 1))
    q10 = at.swap_x(q00)
    q01 = at.swap_core(q00)
    q11 = at.swap_core(q10)

    seqf = sequence.astype(F32)
    h1 = norm(seqf, g1, b1)
    qkv = dot(h1, wqkv).astype(BF)
    att_heads, lse = self_forward(qkv, segc, segr)
    by_x = att_heads.reshape(2, 2, piece, half)
    got = at.swap_x(pick(by_x, 1 - x, 0))
    chip = ordered(x, pick(by_x, x, 0), got, 0)
    got = at.swap_core(pick(chip, 1 - c, 1))
    att = ordered(c, pick(chip, c, 1), got, 2).reshape(tokens, width)

    xin = inputs.reshape(tokens, width).astype(F32)
    x1 = xin + dot(att, wao)
    h2 = norm(x1, g2, b2)
    cq = dot(h2, wcq).astype(BF)
    nb = neighbours.reshape(-1, width)
    ckv = dot(nb, wckv).astype(BF)
    cro = cross_forward(cq, ckv)
    x2 = x1 + dot(cro, wco)
    h3 = norm(x2, g3, b3)
    dy = out_grad.reshape(tokens, width)
    y, dh3, own_grads = feed_forward(h3, dy, [q00, q10])
    y, dh3, far_grads = feed_forward(h3, dy, [q01, q11], (y, dh3))
    outputs = (x2 + y).astype(BF).reshape(seqs, piece, width)

    f0 = at.swap_core(far_grads[0])
    f1 = at.swap_core(far_grads[1])
    away = (own_grads[1].astype(F32) + f1.astype(F32)).astype(BF)
    ffn_sum = own_grads[0].astype(F32) + f0.astype(F32) + at.swap_x(away).astype(F32)
    ffn_own = at.scatter(ffn_sum.reshape(at.n, rows, 2 * width)).astype(BF)
    ffn_x = ordered(x, ffn_own, at.swap_x(ffn_own), 0)
    ffn_all = ordered(c, ffn_x, at.swap_core(ffn_x), 1).reshape(4, rows, 2 * width).astype(F32)
    grad_up = ffn_all[:, :, :width].reshape(4, rows, -1, unit).transpose(1, 2, 0, 3).reshape(rows, -1)
    grad_down = ffn_all[:, :, width:].reshape(4 * unit, width)

    dv3, gg3, gb3 = norm_back(x2, g3, dh3)
    dx2 = dy.astype(F32) + dv3
    dc = dx2.astype(BF)
    grad_co = dot_tn(cro, dc).astype(BF)
    dcro = dot_nt(dc, wco).astype(BF)
    dcq, dckv = cross_backward(cq, ckv, dcro)
    grad_cq = dot_tn(h2, dcq).astype(BF)
    dh2 = dot_nt(dcq, wcq)
    grad_ckv = dot_tn(nb, dckv).astype(BF)
    neighbour_grad = dot_nt(dckv, wckv)
    dv2, gg2, gb2 = norm_back(x1, g2, dh2)
    dx1 = dx2 + dv2
    da = dx1.astype(BF)
    grad_ao = dot_tn(att, da).astype(BF)
    datt = dot_nt(da, wao).astype(BF)

    datt = datt.reshape(seqs, piece, 2, half)
    got = at.swap_core(pick(datt, 1 - c, 2))
    chip = ordered(c, pick(datt, c, 2), got, 1)
    got = at.swap_x(pick(chip, 1 - x, 0))
    do = ordered(x, pick(chip, x, 0), got, 0).reshape(4 * piece, half)
    dqkv = jnp.concatenate(self_backward(qkv, do, segc, segr, lse), 1)
    grad_qkv = dot_tn(h1, dqkv).astype(BF)
    part = dot_nt(dqkv, wqkv).astype(BF).reshape(2, 2, piece, width)
    got = at.swap_core(pick(part, 1 - c, 1))
    chip = (pick(part, c, 1).astype(F32) + got.astype(F32)).astype(BF)
    got = at.swap_x(pick(chip, 1 - x, 0))
    dh1 = ordered(x, pick(chip, x, 0), got, 0).reshape(tokens, width).astype(F32)
    dv1, gg1, gb1 = norm_back(xin, g1, dh1)
    input_grad = (dx1 + dv1).reshape(seqs, piece, width)

    def reduce_halves(halves_sent, halves_kept):
        got = at.swap_core(halves_sent)
        blocks = halves_kept.astype(F32) + got.astype(F32)
        return finish(blocks)

    def finish(blocks):
        own = at.scatter(blocks.reshape(at.n, rows, -1))
        return own + at.swap_x(own.astype(BF)).astype(F32)

    def halves(grad, which):
        return lax.dynamic_slice_in_dim(grad, which * (grad.shape[1] // 2), grad.shape[1] // 2, 1)

    def joined(own, other):
        return ordered(c, own, other, 1).reshape(rows, -1)

    three = (grad_ckv, grad_cq, grad_co)
    own_b = reduce_halves(
        jnp.concatenate([halves(g, 1 - c) for g in three], 1),
        jnp.concatenate([halves(g, c) for g in three], 1),
    )
    far_b = at.swap_core(own_b.astype(BF)).astype(F32)
    out_ckv = joined(own_b[:, :width], far_b[:, :width])
    out_cq = joined(own_b[:, width : width + half], far_b[:, width : width + half])
    out_co = joined(own_b[:, width + half :], far_b[:, width + half :])

    vec = jnp.stack([gg1, gb1, gg2, gb2, gg3, gb3], 1)
    vec = vec + at.swap_core(vec)
    vec = jnp.pad(vec, ((0, 0), (0, 128 - 6)))
    kept_ao = halves(grad_ao, c).astype(F32) + at.swap_core(halves(grad_ao, 1 - c)).astype(F32)
    own_a = finish(jnp.concatenate([grad_qkv.astype(F32), kept_ao, vec], 1))
    far_a = at.swap_core(own_a[:, : 4 * half].astype(BF)).astype(F32)
    out_qkv = ordered(
        c, own_a[:, : 3 * half].reshape(rows, 3, half), far_a[:, : 3 * half].reshape(rows, 3, half), 2
    ).reshape(rows, 6 * half)
    out_ao = joined(own_a[:, 3 * half : 4 * half], far_a[:, 3 * half :])
    vecs = own_a[:, 4 * half : 4 * half + 6].T

    return (
        outputs, input_grad, neighbour_grad.reshape(neighbours.shape),
        vecs[0], vecs[1], out_qkv, out_ao, vecs[2], vecs[3], out_cq, out_ckv, out_co,
        vecs[4], vecs[5], grad_up, grad_down,
    )


def solution(mesh):
    row, mat = P("fsdp"), P("fsdp", None)
    tok, mem = P("fsdp", "seq", None), P("fsdp", "seq", None, None)
    weights = (row, row, mat, mat, row, row, mat, mat, mat, row, row, mat, mat)
    return jax.shard_map(
        per_device,
        mesh=mesh,
        in_specs=(tok, mat, mem, *weights, tok),
        out_specs=(tok, tok, mem, *weights),
        check_vma=False,
    )
```

```python
import functools

import jax
import jax.numpy as jnp
from jax import lax
from jax.experimental import pallas as pl
from jax.experimental.pallas import tpu as pltpu
from jax.sharding import PartitionSpec as P

HEADS = 12
HEAD_DIM = 64
SPAN = 64
EPS = 1e-05
NEG = -1e30
WINDOW = 512
SCALE = HEAD_DIM ** (-0.5)
BF = jnp.bfloat16
F32 = jnp.float32
LIMIT = 60 * 1024 * 1024

GELU_A = 0.7978845608028654
GELU_B = 0.044715


def dot(a, b):
    return lax.dot_general(a, b, (((1,), (0,)), ((), ())), preferred_element_type=F32)


def dot_nt(a, b):
    return lax.dot_general(a, b, (((1,), (1,)), ((), ())), preferred_element_type=F32)


def dot_tn(a, b):
    return lax.dot_general(a, b, (((0,), (0,)), ((), ())), preferred_element_type=F32)


def params(**kw):
    return pltpu.CompilerParams(vmem_limit_bytes=LIMIT, **kw)


def head_mask(rows, head):
    lane = lax.broadcasted_iota(jnp.int32, (rows, 2 * HEAD_DIM), 1)
    return (lane < HEAD_DIM) if head == 0 else (lane >= HEAD_DIM)


def allowed_keys(segc_ref, segr_ref, k0, k1, q0, q1):
    same = segc_ref[k0:k1, :] == segr_ref[:, q0:q1]
    kpos = lax.broadcasted_iota(jnp.int32, (k1 - k0, q1 - q0), 0) + k0
    qpos = lax.broadcasted_iota(jnp.int32, (k1 - k0, q1 - q0), 1) + q0
    return same & (kpos <= qpos)


def self_fwd_kernel(q_ref, k_ref, v_ref, segc_ref, segr_ref, o_ref, lse_ref, vt_ref, *, block):
    length = q_ref.shape[0]
    vt_ref[...] = v_ref[...].astype(F32).T.astype(BF)
    row = lax.broadcasted_iota(jnp.int32, (2 * HEAD_DIM, block), 0)
    for q0 in range(0, length, block):
        q1 = q0 + block
        k0 = max(0, q0 - WINDOW)
        keep = allowed_keys(segc_ref, segr_ref, k0, q1, q0, q1)
        q = q_ref[q0:q1, :]
        outs = []
        for head in range(2):
            qh = jnp.where(head_mask(block, head), q * SCALE, 0).astype(BF)
            s = jnp.where(keep, dot_nt(k_ref[k0:q1, :], qh), NEG)
            top = jnp.max(s, 0, keepdims=True)
            e = jnp.exp(s - top)
            total = jnp.sum(e, 0, keepdims=True)
            outs.append(dot(vt_ref[:, k0:q1], e.astype(BF)) / total)
            lse_ref[0, head : head + 1, q0:q1] = top + jnp.log(total)
        o = jnp.where(row < HEAD_DIM, outs[0], outs[1])
        o_ref[q0:q1, :] = o.T.astype(BF)


def self_forward(qkv, segc, segr):
    length, width = qkv.shape
    pairs = width // (6 * HEAD_DIM)
    pair = 2 * HEAD_DIM
    return pl.pallas_call(
        functools.partial(self_fwd_kernel, block=256),
        grid=(pairs,),
        in_specs=[
            pl.BlockSpec((length, pair), lambda j: (0, j)),
            pl.BlockSpec((length, pair), lambda j: (0, pairs + j)),
            pl.BlockSpec((length, pair), lambda j: (0, 2 * pairs + j)),
            pl.BlockSpec((length, 1), lambda j: (0, 0)),
            pl.BlockSpec((1, length), lambda j: (0, 0)),
        ],
        out_specs=[
            pl.BlockSpec((length, pair), lambda j: (0, j)),
            pl.BlockSpec((1, 8, length), lambda j: (j, 0, 0)),
        ],
        out_shape=[
            jax.ShapeDtypeStruct((length, pairs * pair), BF),
            jax.ShapeDtypeStruct((pairs, 8, length), F32),
        ],
        scratch_shapes=[pltpu.VMEM((pair, length), BF)],
        compiler_params=params(),
        cost_estimate=pl.CostEstimate(
            flops=8 * pairs * length * length * HEAD_DIM,
            bytes_accessed=10 * length * pairs * pair,
            transcendentals=2 * pairs * length * length // 2,
        ),
        name="self_forward",
    )(qkv, qkv, qkv, segc, segr)


def self_bwd_kernel(
    q_ref, k_ref, v_ref, do_ref, segc_ref, segr_ref, lse_ref, dq_ref, dk_ref, dv_ref, kt_ref, dka, dva, *, block
):
    length = q_ref.shape[0]
    kt_ref[...] = k_ref[...].astype(F32).T.astype(BF)
    dka[...] = jnp.zeros_like(dka)
    dva[...] = jnp.zeros_like(dva)
    row = lax.broadcasted_iota(jnp.int32, (2 * HEAD_DIM, block), 0)
    for q0 in range(0, length, block):
        q1 = q0 + block
        k0 = max(0, q0 - WINDOW)
        keep = allowed_keys(segc_ref, segr_ref, k0, q1, q0, q1)
        q = q_ref[q0:q1, :]
        do = do_ref[q0:q1, :]
        dqs = []
        for head in range(2):
            mine = head_mask(block, head)
            qh = jnp.where(mine, q * SCALE, 0).astype(BF)
            doh = jnp.where(mine, do, 0).astype(BF)
            s = jnp.where(keep, dot_nt(k_ref[k0:q1, :], qh), NEG)
            p = jnp.exp(s - lse_ref[0, head : head + 1, q0:q1])
            dp = dot_nt(v_ref[k0:q1, :], doh)
            delta = jnp.sum(p * dp, 0, keepdims=True)
            ds = (p * (dp - delta)).astype(BF)
            dka[k0:q1, :] += dot(ds, qh)
            dva[k0:q1, :] += dot(p.astype(BF), doh)
            dqs.append(dot(kt_ref[:, k0:q1], ds))
        dq = jnp.where(row < HEAD_DIM, dqs[0], dqs[1]) * SCALE
        dq_ref[q0:q1, :] = dq.T.astype(BF)
    dk_ref[...] = dka[...].astype(BF)
    dv_ref[...] = dva[...].astype(BF)


def self_backward(qkv, do, segc, segr, lse):
    length, width = qkv.shape
    pairs = width // (6 * HEAD_DIM)
    pair = 2 * HEAD_DIM
    column = pl.BlockSpec((length, pair), lambda j: (0, j))
    return pl.pallas_call(
        functools.partial(self_bwd_kernel, block=256),
        grid=(pairs,),
        in_specs=[
            column,
            pl.BlockSpec((length, pair), lambda j: (0, pairs + j)),
            pl.BlockSpec((length, pair), lambda j: (0, 2 * pairs + j)),
            column,
            pl.BlockSpec((length, 1), lambda j: (0, 0)),
            pl.BlockSpec((1, length), lambda j: (0, 0)),
            pl.BlockSpec((1, 8, length), lambda j: (j, 0, 0)),
        ],
        out_specs=[column] * 3,
        out_shape=[jax.ShapeDtypeStruct((length, pairs * pair), BF)] * 3,
        scratch_shapes=[
            pltpu.VMEM((pair, length), BF),
            pltpu.VMEM((length, pair), F32),
            pltpu.VMEM((length, pair), F32),
        ],
        compiler_params=params(),
        cost_estimate=pl.CostEstimate(
            flops=20 * pairs * length * length * HEAD_DIM,
            bytes_accessed=16 * length * pairs * pair,
            transcendentals=pairs * length * length,
        ),
        name="self_backward",
    )(qkv, qkv, qkv, do, segc, segr, lse)


def stack_heads(block):
    rows = block.shape[0]
    return jnp.concatenate(
        [jnp.where(head_mask(rows, head), block, 0) for head in range(2)], 0
    ).astype(BF)


def unstack_heads(block):
    rows = block.shape[0] // 2
    return jnp.where(head_mask(rows, 0), block[:rows], block[rows:])


def cross_weights(k, qs):
    s = dot_nt(k, qs)
    e = jnp.exp(s - jnp.max(s, 0, keepdims=True))
    return e, jnp.sum(e, 0, keepdims=True)


def cross_fwd_kernel(q_ref, k_ref, v_ref, o_ref):
    pair = 2 * HEAD_DIM
    for at in range(0, q_ref.shape[1], pair):
        cols = slice(at, at + pair)
        qs = stack_heads(q_ref[:, cols] * SCALE)
        e, total = cross_weights(k_ref[:, cols], qs)
        o = dot_tn((e / total).astype(BF), v_ref[:, cols])
        o_ref[:, cols] = unstack_heads(o).astype(BF)


def cross_forward(cq, ckv):
    tokens, width = cq.shape
    spans = tokens // SPAN
    memory = ckv.shape[0] // spans
    return pl.pallas_call(
        cross_fwd_kernel,
        grid=(spans,),
        in_specs=[
            pl.BlockSpec((SPAN, width), lambda i: (i, 0)),
            pl.BlockSpec((memory, width), lambda i: (i, 0)),
            pl.BlockSpec((memory, width), lambda i: (i, 1)),
        ],
        out_specs=pl.BlockSpec((SPAN, width), lambda i: (i, 0)),
        out_shape=jax.ShapeDtypeStruct((tokens, width), BF),
        compiler_params=params(),
        cost_estimate=pl.CostEstimate(
            flops=4 * tokens * memory * width,
            bytes_accessed=4 * tokens * width + 4 * spans * memory * width,
            transcendentals=tokens * memory * HEADS,
        ),
        name="cross_forward",
    )(cq, ckv, ckv)


def cross_bwd_kernel(q_ref, k_ref, v_ref, do_ref, dq_ref, dkv_ref):
    pair = 2 * HEAD_DIM
    width = q_ref.shape[1]
    for at in range(0, width, pair):
        cols = slice(at, at + pair)
        qs = stack_heads(q_ref[:, cols] * SCALE)
        dos = stack_heads(do_ref[:, cols])
        k = k_ref[:, cols]
        e, total = cross_weights(k, qs)
        p = e / total
        dp = dot_nt(v_ref[:, cols], dos)
        delta = jnp.sum(p * dp, 0, keepdims=True)
        ds = (p * (dp - delta)).astype(BF)
        dq_ref[:, cols] = (unstack_heads(dot_tn(ds, k)) * SCALE).astype(BF)
        dkv_ref[:, cols] = dot(ds, qs).astype(BF)
        dkv_ref[:, width + at : width + at + pair] = dot(p.astype(BF), dos).astype(BF)


def cross_backward(cq, ckv, do):
    tokens, width = cq.shape
    spans = tokens // SPAN
    memory = ckv.shape[0] // spans
    return pl.pallas_call(
        cross_bwd_kernel,
        grid=(spans,),
        in_specs=[
            pl.BlockSpec((SPAN, width), lambda i: (i, 0)),
            pl.BlockSpec((memory, width), lambda i: (i, 0)),
            pl.BlockSpec((memory, width), lambda i: (i, 1)),
            pl.BlockSpec((SPAN, width), lambda i: (i, 0)),
        ],
        out_specs=[
            pl.BlockSpec((SPAN, width), lambda i: (i, 0)),
            pl.BlockSpec((memory, 2 * width), lambda i: (i, 0)),
        ],
        out_shape=[
            jax.ShapeDtypeStruct((tokens, width), BF),
            jax.ShapeDtypeStruct((spans * memory, 2 * width), BF),
        ],
        compiler_params=params(),
        cost_estimate=pl.CostEstimate(
            flops=10 * tokens * memory * width,
            bytes_accessed=6 * tokens * width + 8 * spans * memory * width,
            transcendentals=tokens * memory * HEADS,
        ),
        name="cross_backward",
    )(cq, ckv, ckv, do)


def ffn_kernel(h_ref, dy_ref, *refs, quarters, carry, chunk):
    ups, downs = refs[:quarters], refs[quarters : 2 * quarters]
    rest = refs[2 * quarters :]
    if carry:
        y0_ref, dh0_ref, rest = rest[0], rest[1], rest[2:]
    y_ref, dh_ref = rest[0], rest[1]
    grads = rest[2:]
    step = pl.program_id(0)
    width = h_ref.shape[1]

    @pl.when(step == 0)
    def _():
        y_ref[...] = y0_ref[...] if carry else jnp.zeros_like(y_ref)
        dh_ref[...] = dh0_ref[...] if carry else jnp.zeros_like(dh_ref)

    h = h_ref[...]
    dy = dy_ref[...]
    at = pl.multiple_of(step * chunk, chunk)
    for up_ref, down_ref, g_ref in zip(ups, downs, grads):
        up, down = up_ref[...], down_ref[...]
        u = dot(h, up)
        t = jnp.tanh(GELU_A * (u + GELU_B * (u * u * u)))
        gl = (0.5 * u * (1.0 + t)).astype(BF)
        y_ref[...] += dot(gl, down)
        slope = 0.5 * (1.0 + t) + 0.5 * u * (1.0 - t * t) * (GELU_A * (1.0 + 3.0 * GELU_B * (u * u)))
        du = (dot_nt(dy, down) * slope).astype(BF)
        dh_ref[...] += dot_nt(du, up)
        g_ref[:, pl.ds(at, chunk)] = dot_tn(h, du).astype(BF)
        g_ref[pl.ds(at, chunk), pl.ds(width, width)] = dot_tn(gl, dy).astype(BF)


def feed_forward(h, dy, weights, carry=None):
    tokens, width = h.shape
    n = len(weights)
    hidden = weights[0].shape[0]
    chunk = 256
    whole = pl.BlockSpec((tokens, width), lambda j: (0, 0))
    operands = [h, dy, *weights, *weights]
    in_specs = [whole, whole]
    in_specs += [pl.BlockSpec((width, chunk), lambda j: (0, j))] * n
    in_specs += [pl.BlockSpec((chunk, width), lambda j: (j, 1))] * n
    if carry is not None:
        operands += list(carry)
        in_specs += [whole, whole]
    out = pl.pallas_call(
        functools.partial(ffn_kernel, quarters=n, carry=carry is not None, chunk=chunk),
        grid=(hidden // chunk,),
        in_specs=in_specs,
        out_specs=[whole, whole] + [pl.BlockSpec((hidden, 2 * width), lambda j: (0, 0))] * n,
        out_shape=[jax.ShapeDtypeStruct((tokens, width), F32)] * 2
        + [jax.ShapeDtypeStruct((hidden, 2 * width), BF)] * n,
        compiler_params=params(),
        cost_estimate=pl.CostEstimate(
            flops=12 * n * tokens * width * hidden,
            bytes_accessed=8 * n * width * hidden + 16 * tokens * width,
            transcendentals=n * tokens * hidden,
        ),
        name="feed_forward",
    )(*operands)
    return out[0], out[1], out[2:]


def assemble_kernel(idx_ref, *refs, counts, rows):
    pieces, out_ref, sem = refs[: len(counts)], refs[len(counts)], refs[len(counts) + 1]
    copies = []
    for piece, count in zip(pieces, counts):
        for j in range(count):
            i = len(copies)
            at = pl.multiple_of(idx_ref[i] * rows, rows)
            copies.append(
                pltpu.make_async_copy(
                    piece.at[pl.ds(j * rows, rows), :], out_ref.at[pl.ds(at, rows), :], sem.at[i]
                )
            )
    for copy in copies:
        copy.start()
    for copy in copies:
        copy.wait()


def assemble(pieces, places, rows):
    counts = [p.shape[0] // rows for p in pieces]
    cols, n = pieces[0].shape[1], sum(counts)
    return pl.pallas_call(
        functools.partial(assemble_kernel, counts=counts, rows=rows),
        grid_spec=pltpu.PrefetchScalarGridSpec(
            num_scalar_prefetch=1,
            grid=(1,),
            in_specs=[pl.BlockSpec(memory_space=pl.ANY)] * len(pieces),
            out_specs=pl.BlockSpec((n * rows, cols), lambda i, idx: (0, 0)),
            scratch_shapes=[pltpu.SemaphoreType.DMA((n,))],
        ),
        out_shape=jax.ShapeDtypeStruct((n * rows, cols), pieces[0].dtype),
        compiler_params=params(),
        cost_estimate=pl.CostEstimate(
            flops=0, bytes_accessed=4 * n * rows * cols, transcendentals=0
        ),
        name="assemble",
    )(jnp.stack(places).astype(jnp.int32), *pieces)


def merge_kernel(c_ref, own_ref, far_ref, *refs, sizes):
    outs, sem = refs[:-1], refs[-1]
    copies, start = [], 0
    for out_ref, size in zip(outs, sizes):
        for source, side in ((own_ref, c_ref[0]), (far_ref, 1 - c_ref[0])):
            at = pl.multiple_of(side * size, size)
            copies.append(
                pltpu.make_async_copy(
                    source.at[:, pl.ds(start, size)], out_ref.at[:, pl.ds(at, size)], sem.at[len(copies)]
                )
            )
        start += size
    for copy in copies:
        copy.start()
    for copy in copies:
        copy.wait()


def merge(own, far, c, sizes):
    rows = own.shape[0]
    return pl.pallas_call(
        functools.partial(merge_kernel, sizes=sizes),
        grid_spec=pltpu.PrefetchScalarGridSpec(
            num_scalar_prefetch=1,
            grid=(1,),
            in_specs=[pl.BlockSpec(memory_space=pl.ANY)] * 2,
            out_specs=[pl.BlockSpec((rows, 2 * n), lambda i, idx: (0, 0)) for n in sizes],
            scratch_shapes=[pltpu.SemaphoreType.DMA((2 * len(sizes),))],
        ),
        out_shape=[jax.ShapeDtypeStruct((rows, 2 * n), own.dtype) for n in sizes],
        compiler_params=params(),
        cost_estimate=pl.CostEstimate(
            flops=0, bytes_accessed=8 * rows * sum(sizes), transcendentals=0
        ),
        name="merge",
    )(c.reshape(1).astype(jnp.int32), own, far)


def join_kernel(c_ref, own_ref, far_ref, *outs, layout, size):
    start = 0
    for out_ref, segments, width in layout_refs(outs, layout):
        for j in range(segments):
            for source, side in ((own_ref, c_ref[0]), (far_ref, 1 - c_ref[0])):
                at = pl.multiple_of(side * width, size)
                out_ref[:, pl.ds(at + 2 * j * width, width)] = source[:, start : start + width].astype(F32)
            start += width


def layout_refs(outs, layout):
    return [(o, n, w) for o, (n, w) in zip(outs, layout)]


def join(own, far, c, layout):
    rows = own.shape[0]
    shapes = [jax.ShapeDtypeStruct((rows, 2 * n * w), F32) for n, w in layout]
    return pl.pallas_call(
        functools.partial(join_kernel, layout=layout, size=128),
        grid_spec=pltpu.PrefetchScalarGridSpec(
            num_scalar_prefetch=1,
            grid=(1,),
            in_specs=[pl.BlockSpec(v.shape, lambda i, idx: (0, 0)) for v in (own, far)],
            out_specs=[pl.BlockSpec(v.shape, lambda i, idx: (0, 0)) for v in shapes],
        ),
        out_shape=shapes,
        compiler_params=params(),
        name="join",
    )(c.reshape(1).astype(jnp.int32), own, far)


def spread_kernel(p_ref, up_ref, down_ref, *, unit):
    quarters, rows, cols = p_ref.shape
    width = cols // 2
    for s in range(quarters):
        for f in range(width // unit):
            up_ref[:, (f * quarters + s) * unit : (f * quarters + s + 1) * unit] = p_ref[
                s, :, f * unit : (f + 1) * unit
            ].astype(F32)
        down_ref[s * rows : (s + 1) * rows, :] = p_ref[s, :, width:].astype(F32)


def spread(pieces, unit):
    quarters, rows, cols = pieces.shape
    return pl.pallas_call(
        functools.partial(spread_kernel, unit=unit),
        out_shape=[
            jax.ShapeDtypeStruct((rows, quarters * cols // 2), F32),
            jax.ShapeDtypeStruct((quarters * rows, cols // 2), F32),
        ],
        compiler_params=params(),
        name="spread",
    )(pieces)


def grad_kernel(side_ref, a_ref, b_ref, *refs):
    out_ref = refs[-1]
    total = dot_tn(a_ref[...], b_ref[...])
    if len(refs) == 2:
        total = total + refs[0][...].astype(F32)
    out_ref[...] = total.astype(BF)


def grad_half(a, b, side, more=None):
    tokens, rows = a.shape
    cols = b.shape[1] // 2
    block = 384
    blocks = cols // block
    operands = [a, b] + ([] if more is None else [more])
    out_spec = pl.BlockSpec((rows, block), lambda j, side: (0, j))
    return pl.pallas_call(
        grad_kernel,
        grid_spec=pltpu.PrefetchScalarGridSpec(
            num_scalar_prefetch=1,
            grid=(blocks,),
            in_specs=[
                pl.BlockSpec((tokens, rows), lambda j, side: (0, 0)),
                pl.BlockSpec((tokens, block), lambda j, side: (0, side[0] * blocks + j)),
            ]
            + [out_spec] * (len(operands) - 2),
            out_specs=out_spec,
        ),
        out_shape=jax.ShapeDtypeStruct((rows, cols), BF),
        compiler_params=params(),
        cost_estimate=pl.CostEstimate(
            flops=2 * tokens * rows * cols,
            bytes_accessed=2 * tokens * (rows + cols) + 4 * rows * cols,
            transcendentals=0,
        ),
        name="grad_half",
    )(side.reshape(1).astype(jnp.int32), *operands)


class Place:
    def __init__(self):
        self.n = lax.axis_size("fsdp")
        f = lax.axis_index("fsdp")
        s = lax.axis_index("seq")
        self.z, self.y = f // 2, f % 2
        self.x, self.c = s // 2, s % 2
        self.s = s
        self.direct = self.n == 8

    def swap_core(self, value):
        return lax.ppermute(value, "seq", [(0, 1), (1, 0), (2, 3), (3, 2)])

    def swap_x(self, value):
        return lax.ppermute(value, "seq", [(0, 2), (2, 0), (1, 3), (3, 1)])

    def swap_y(self, value):
        return lax.ppermute(value, "fsdp", [(i, i ^ 1) for i in range(self.n)])

    def shift_z(self, value, hops):
        return lax.ppermute(value, "fsdp", [(i, (i + 2 * hops) % self.n) for i in range(self.n)])

    def places(self):
        base = [2 * ((self.z - k) % 4) for k in range(4)]
        return [b + self.y for b in base] + [b + 1 - self.y for b in base]

    def shifts(self, piece):
        return [self.shift_z(piece, k) for k in (1, 2, 3)]

    def send_y(self, mats):
        mats = [m.reshape(self.n // 2, 2, -1, m.shape[1]) for m in mats]
        sent = jnp.concatenate([pick(m, 1 - self.y, 1).astype(BF) for m in mats], 2)
        kept = jnp.concatenate([pick(m, self.y, 1).astype(BF) for m in mats], 2)
        return sent, kept

    def send_z(self, column):
        own = pick(column, self.z, 0)
        if not self.direct:
            total = lax.psum(column, "fsdp")
            return own, [pick(total, self.z, 0)]
        return own, [self.shift_z(pick(column, (self.z + k) % 4, 0), k) for k in (1, 2, 3)]

    def total(self, own, got):
        if not self.direct:
            return got[0].astype(F32)
        return sum((g.astype(F32) for g in got), own.astype(F32))


def tie(*values):
    return lax.optimization_barrier(values)


def added(first, second):
    return (first.astype(F32) + second.astype(F32)).astype(BF)


def pick(value, index, axis):
    return lax.dynamic_index_in_dim(value, index, axis, keepdims=False)


def ordered(flag, first, second, axis):
    low = jnp.where(flag == 0, first, second)
    high = jnp.where(flag == 0, second, first)
    return jnp.stack([low, high], axis)


def norm_stats(values):
    centre = values - jnp.mean(values, -1, keepdims=True)
    r = lax.rsqrt(jnp.mean(centre * centre, -1, keepdims=True) + EPS)
    return centre * r, r


def norm(values, gain, bias):
    xhat, _ = norm_stats(values)
    return (xhat * gain + bias).astype(BF)


def norm_back(values, gain, dh):
    xhat, r = norm_stats(values)
    dg = dh * gain
    dv = r * (
        dg - jnp.mean(dg, -1, keepdims=True) - xhat * jnp.mean(dg * xhat, -1, keepdims=True)
    )
    return dv, jnp.sum(dh * xhat, 0), jnp.sum(dh, 0)


def per_device(
    inputs, segments, neighbours,
    ln1_gain, ln1_bias, w_qkv, w_attn_out, ln2_gain, ln2_bias, cross_q, cross_kv, cross_out,
    ln3_gain, ln3_bias, w_up, w_down, out_grad,
):
    at = Place()
    x, c = at.x, at.c
    seqs, piece, width = inputs.shape
    half = width // 2
    rows = w_qkv.shape[0]
    tokens = seqs * piece

    theirs = at.swap_x(pick(inputs, 1 - x, 0))
    mine = pick(inputs, x, 0)
    blocks = ordered(x, mine, theirs, 0)
    sequence = ordered(c, blocks, at.swap_core(blocks), 1).reshape(4 * piece, width)
    seg = pick(segments, x, 0)
    segc, segr = seg[:, None], seg[None, :]

    vectors = jnp.stack([ln1_gain, ln1_bias, ln2_gain, ln2_bias, ln3_gain, ln3_bias], 1)
    vectors = jnp.pad(vectors, ((0, 0), (0, 128 - vectors.shape[1])))
    piece_a = jnp.concatenate(
        [lax.dynamic_slice_in_dim(w_qkv, j * width + c * half, half, 1) for j in range(3)] + [vectors], 1
    )

    def half_of(weight):
        return lax.dynamic_slice_in_dim(weight, c * (weight.shape[1] // 2), weight.shape[1] // 2, 1)

    piece_b = jnp.concatenate([half_of(w) for w in (cross_kv, w_attn_out, cross_q, cross_out)], 1)
    unit = w_down.shape[0] // 4
    up_quarter = pick(w_up.reshape(rows, -1, 4, unit), at.s, 2).reshape(rows, -1)
    down_quarter = pick(w_down.reshape(4, unit, width), at.s, 0)
    piece_f = jnp.concatenate([up_quarter, down_quarter], 1)
    if at.direct:
        places = at.places()
        first = at.swap_y(piece_a)
        zs, first, piece_f = tie(at.shifts(piece_a), first, piece_f)
        others = at.swap_y(jnp.concatenate(zs, 0))
        zs_f, others, piece_b = tie(at.shifts(piece_f), others, piece_b)
        group_a = assemble([piece_a, *zs, first, others], places, rows)
        column_f = jnp.concatenate([piece_f, *zs_f], 0)
        moving = (at.swap_x(column_f), at.swap_y(column_f), at.shifts(piece_b))
    else:
        group_a = lax.all_gather(piece_a, "fsdp", axis=0, tiled=True)
        moving = ()
    wqkv = group_a[:, : 3 * half]
    gains = group_a[:, 3 * half : 3 * half + 6].T.astype(F32)
    g1, b1, g2, b2, g3, b3 = (gains[i] for i in range(6))

    seqf = sequence.astype(F32)
    h1 = norm(seqf, g1, b1)
    qkv = dot(h1, wqkv).astype(BF)
    qkv, moving = tie(qkv, moving)
    if at.direct:
        xcolumn, others_f, zs_b = moving
        column_b = jnp.concatenate([piece_b, *zs_b], 0)
        moving = (at.swap_x(others_f), at.swap_y(column_b))
    att_heads, lse = self_forward(qkv, segc, segr)
    by_x = att_heads.reshape(2, 2, piece, half)
    got = at.swap_x(pick(by_x, 1 - x, 0))
    chip = ordered(x, pick(by_x, x, 0), got, 0)
    got = at.swap_core(pick(chip, 1 - c, 1))
    att = ordered(c, pick(chip, c, 1), got, 2).reshape(tokens, width)
    att, moving = tie(att, moving)
    if at.direct:
        group_b = assemble([column_b, moving[1]], places, rows)
        q00 = assemble([column_f, others_f], places, rows)
        q10 = assemble([xcolumn, moving[0]], places, rows)
    else:
        group_b = lax.all_gather(piece_b, "fsdp", axis=0, tiled=True)
        q00 = lax.all_gather(piece_f, "fsdp", axis=0, tiled=True)
        q10 = at.swap_x(q00)
    wckv, wao, wcq, wco = merge(group_b, at.swap_core(group_b), c, (width, half, half, half))
    q01 = at.swap_core(q00)
    q11 = at.swap_core(q10)

    xin = inputs.reshape(tokens, width).astype(F32)
    x1 = xin + dot(att, wao)
    h2 = norm(x1, g2, b2)
    cq = dot(h2, wcq).astype(BF)
    nb = neighbours.reshape(-1, width)
    ckv = dot(nb, wckv).astype(BF)
    cro = cross_forward(cq, ckv)
    x2 = x1 + dot(cro, wco)
    h3 = norm(x2, g3, b3)
    dy = out_grad.reshape(tokens, width)
    y, dh3, far_grads = feed_forward(h3, dy, [q01, q11])
    f0 = at.swap_core(far_grads[0])
    f1 = at.swap_core(far_grads[1])
    y, dh3, own_grads = feed_forward(h3, dy, [q00, q10], (y, dh3))
    outputs = (x2 + y).astype(BF).reshape(seqs, piece, width)

    away, dh3 = tie(added(own_grads[1], f1), dh3)
    ffn_got = at.swap_x(away)

    dv3, gg3, gb3 = norm_back(x2, g3, dh3)
    dx2 = dy.astype(F32) + dv3
    dc = dx2.astype(BF)
    dcro = dot_nt(dc, wco).astype(BF)
    dcq, dckv = cross_backward(cq, ckv, dcro)
    dh2 = dot_nt(dcq, wcq)
    dv2, gg2, gb2 = norm_back(x1, g2, dh2)
    dx1 = dx2 + dv2
    da = dx1.astype(BF)
    datt = dot_nt(da, wao).astype(BF)
    pairs = ((nb, dckv), (att, da), (h2, dcq), (cro, dc))
    sent_b = [grad_half(a, b, 1 - c) for a, b in pairs]
    sums_b = [grad_half(a, b, c, at.swap_core(v)) for (a, b), v in zip(pairs, sent_b)]
    sent_b, kept_b = at.send_y(sums_b)
    neighbour_grad = dot_nt(dckv, wckv)

    datt = datt.reshape(seqs, piece, 2, half)
    got = at.swap_core(pick(datt, 1 - c, 2))
    chip = ordered(c, pick(datt, c, 2), got, 1)
    chip, ffn_got = tie(chip, ffn_got)
    got = at.swap_x(pick(chip, 1 - x, 0))
    do = ordered(x, pick(chip, x, 0), got, 0).reshape(4 * piece, half)
    ffn_sum = own_grads[0].astype(F32) + f0.astype(F32) + ffn_got.astype(F32)
    sent_f, kept_f = at.send_y([ffn_sum.astype(BF)])
    do, sent_b, sent_f = tie(do, sent_b, sent_f)
    got_f, got_b = at.swap_y(sent_f), at.swap_y(sent_b)
    dqkv = jnp.concatenate(self_backward(qkv, do, segc, segr, lse), 1)
    dqkv, got_f = tie(dqkv, got_f)
    moving_f = at.send_z(added(kept_f, got_f))
    grad_qkv = dot_tn(h1, dqkv).astype(BF)
    sent_a, kept_a = at.send_y([grad_qkv])
    part = dot_nt(dqkv, wqkv).astype(BF).reshape(2, 2, piece, width)
    part, sent_a, got_b = tie(part, sent_a, got_b)
    got_a = at.swap_y(sent_a)
    moving_b = at.send_z(added(kept_b, got_b))
    got = at.swap_core(pick(part, 1 - c, 1))
    chip = (pick(part, c, 1).astype(F32) + got.astype(F32)).astype(BF)
    got = at.swap_x(pick(chip, 1 - x, 0))
    dh1 = ordered(x, pick(chip, x, 0), got, 0).reshape(tokens, width).astype(F32)
    dv1, gg1, gb1 = norm_back(xin, g1, dh1)
    input_grad = (dx1 + dv1).reshape(seqs, piece, width)

    def finish(own):
        return own + at.swap_x(own.astype(BF)).astype(F32)

    input_grad, moving_f, got_a = tie(input_grad, moving_f, got_a)
    vec = jnp.pad(jnp.stack([gg1, gb1, gg2, gb2, gg3, gb3], 1), ((0, 0), (0, 128 - 6)))
    vec = vec + at.swap_core(vec)
    vec = pick((vec + at.swap_y(vec)).reshape(at.n // 2, 2, rows, 128), at.y, 1).astype(BF)
    moving_a = at.send_z(jnp.concatenate([added(kept_a, got_a), vec], 2))
    ffn_own = at.total(*moving_f).astype(BF)
    ffn_x = ordered(x, ffn_own, at.swap_x(ffn_own), 0)
    ffn_all = ordered(c, ffn_x, at.swap_core(ffn_x), 1).reshape(4, rows, 2 * width)
    grad_up, grad_down = spread(ffn_all, unit)
    own_b = finish(at.total(*moving_b))
    far_b = at.swap_core(own_b.astype(BF))
    out_ckv, out_ao, out_cq, out_co = join(
        own_b, far_b, c, ((1, width), (1, half), (1, half), (1, half))
    )
    own_a = finish(at.total(*moving_a))
    far_a = at.swap_core(own_a[:, : 3 * half].astype(BF))
    (out_qkv,) = join(own_a, far_a, c, ((3, half),))
    vecs = own_a[:, 3 * half : 3 * half + 6].T

    return (
        outputs, input_grad, neighbour_grad.reshape(neighbours.shape),
        vecs[0], vecs[1], out_qkv, out_ao, vecs[2], vecs[3], out_cq, out_ckv, out_co,
        vecs[4], vecs[5], grad_up, grad_down,
    )


def solution(mesh):
    row, mat = P("fsdp"), P("fsdp", None)
    tok, mem = P("fsdp", "seq", None), P("fsdp", "seq", None, None)
    weights = (row, row, mat, mat, row, row, mat, mat, mat, row, row, mat, mat)
    return jax.shard_map(
        per_device,
        mesh=mesh,
        in_specs=(tok, mat, mem, *weights, tok),
        out_specs=(tok, tok, mem, *weights),
        check_vma=False,
    )
```

```python
import functools

import jax
import jax.numpy as jnp
from jax import lax
from jax.experimental import pallas as pl
from jax.experimental.pallas import tpu as pltpu
from jax.sharding import PartitionSpec as P

HEADS = 12
HEAD_DIM = 64
SPAN = 64
EPS = 1e-05
NEG = -1e30
WINDOW = 512
SCALE = HEAD_DIM ** (-0.5)
BF = jnp.bfloat16
F32 = jnp.float32
LIMIT = 60 * 1024 * 1024

GELU_A = 0.7978845608028654
GELU_B = 0.044715


def dot(a, b):
    return lax.dot_general(a, b, (((1,), (0,)), ((), ())), preferred_element_type=F32)


def dot_nt(a, b):
    return lax.dot_general(a, b, (((1,), (1,)), ((), ())), preferred_element_type=F32)


def dot_tn(a, b):
    return lax.dot_general(a, b, (((0,), (0,)), ((), ())), preferred_element_type=F32)


def params(**kw):
    return pltpu.CompilerParams(vmem_limit_bytes=LIMIT, **kw)


def head_mask(rows, head):
    lane = lax.broadcasted_iota(jnp.int32, (rows, 2 * HEAD_DIM), 1)
    return (lane < HEAD_DIM) if head == 0 else (lane >= HEAD_DIM)


def allowed_keys(segc_ref, segr_ref, k0, k1, q0, q1):
    same = segc_ref[k0:k1, :] == segr_ref[:, q0:q1]
    kpos = lax.broadcasted_iota(jnp.int32, (k1 - k0, q1 - q0), 0) + k0
    qpos = lax.broadcasted_iota(jnp.int32, (k1 - k0, q1 - q0), 1) + q0
    return same & (kpos <= qpos)


def self_fwd_kernel(q_ref, k_ref, v_ref, segc_ref, segr_ref, o_ref, lse_ref, vt_ref, *, block):
    length = q_ref.shape[0]
    vt_ref[...] = v_ref[...].astype(F32).T.astype(BF)
    row = lax.broadcasted_iota(jnp.int32, (2 * HEAD_DIM, block), 0)
    for q0 in range(0, length, block):
        q1 = q0 + block
        k0 = max(0, q0 - WINDOW)
        keep = allowed_keys(segc_ref, segr_ref, k0, q1, q0, q1)
        q = q_ref[q0:q1, :]
        outs = []
        for head in range(2):
            qh = jnp.where(head_mask(block, head), q * SCALE, 0).astype(BF)
            s = jnp.where(keep, dot_nt(k_ref[k0:q1, :], qh), NEG)
            top = jnp.max(s, 0, keepdims=True)
            e = jnp.exp(s - top)
            total = jnp.sum(e, 0, keepdims=True)
            outs.append(dot(vt_ref[:, k0:q1], e.astype(BF)) / total)
            lse_ref[0, head : head + 1, q0:q1] = top + jnp.log(total)
        o = jnp.where(row < HEAD_DIM, outs[0], outs[1])
        o_ref[q0:q1, :] = o.T.astype(BF)


def self_forward(qkv, segc, segr):
    length, width = qkv.shape
    pairs = width // (6 * HEAD_DIM)
    pair = 2 * HEAD_DIM
    return pl.pallas_call(
        functools.partial(self_fwd_kernel, block=256),
        grid=(pairs,),
        in_specs=[
            pl.BlockSpec((length, pair), lambda j: (0, j)),
            pl.BlockSpec((length, pair), lambda j: (0, pairs + j)),
            pl.BlockSpec((length, pair), lambda j: (0, 2 * pairs + j)),
            pl.BlockSpec((length, 1), lambda j: (0, 0)),
            pl.BlockSpec((1, length), lambda j: (0, 0)),
        ],
        out_specs=[
            pl.BlockSpec((length, pair), lambda j: (0, j)),
            pl.BlockSpec((1, 8, length), lambda j: (j, 0, 0)),
        ],
        out_shape=[
            jax.ShapeDtypeStruct((length, pairs * pair), BF),
            jax.ShapeDtypeStruct((pairs, 8, length), F32),
        ],
        scratch_shapes=[pltpu.VMEM((pair, length), BF)],
        compiler_params=params(),
        cost_estimate=pl.CostEstimate(
            flops=8 * pairs * length * length * HEAD_DIM,
            bytes_accessed=10 * length * pairs * pair,
            transcendentals=2 * pairs * length * length // 2,
        ),
        name="self_forward",
    )(qkv, qkv, qkv, segc, segr)


def self_bwd_kernel(
    q_ref, k_ref, v_ref, do_ref, segc_ref, segr_ref, lse_ref, dq_ref, dk_ref, dv_ref, kt_ref, dka, dva, *, block
):
    length = q_ref.shape[0]
    kt_ref[...] = k_ref[...].astype(F32).T.astype(BF)
    dka[...] = jnp.zeros_like(dka)
    dva[...] = jnp.zeros_like(dva)
    row = lax.broadcasted_iota(jnp.int32, (2 * HEAD_DIM, block), 0)
    for q0 in range(0, length, block):
        q1 = q0 + block
        k0 = max(0, q0 - WINDOW)
        keep = allowed_keys(segc_ref, segr_ref, k0, q1, q0, q1)
        q = q_ref[q0:q1, :]
        do = do_ref[q0:q1, :]
        dqs = []
        for head in range(2):
            mine = head_mask(block, head)
            qh = jnp.where(mine, q * SCALE, 0).astype(BF)
            doh = jnp.where(mine, do, 0).astype(BF)
            s = jnp.where(keep, dot_nt(k_ref[k0:q1, :], qh), NEG)
            p = jnp.exp(s - lse_ref[0, head : head + 1, q0:q1])
            dp = dot_nt(v_ref[k0:q1, :], doh)
            delta = jnp.sum(p * dp, 0, keepdims=True)
            ds = (p * (dp - delta)).astype(BF)
            dka[k0:q1, :] += dot(ds, qh)
            dva[k0:q1, :] += dot(p.astype(BF), doh)
            dqs.append(dot(kt_ref[:, k0:q1], ds))
        dq = jnp.where(row < HEAD_DIM, dqs[0], dqs[1]) * SCALE
        dq_ref[q0:q1, :] = dq.T.astype(BF)
    dk_ref[...] = dka[...].astype(BF)
    dv_ref[...] = dva[...].astype(BF)


def self_backward(qkv, do, segc, segr, lse):
    length, width = qkv.shape
    pairs = width // (6 * HEAD_DIM)
    pair = 2 * HEAD_DIM
    column = pl.BlockSpec((length, pair), lambda j: (0, j))
    return pl.pallas_call(
        functools.partial(self_bwd_kernel, block=256),
        grid=(pairs,),
        in_specs=[
            column,
            pl.BlockSpec((length, pair), lambda j: (0, pairs + j)),
            pl.BlockSpec((length, pair), lambda j: (0, 2 * pairs + j)),
            column,
            pl.BlockSpec((length, 1), lambda j: (0, 0)),
            pl.BlockSpec((1, length), lambda j: (0, 0)),
            pl.BlockSpec((1, 8, length), lambda j: (j, 0, 0)),
        ],
        out_specs=[column] * 3,
        out_shape=[jax.ShapeDtypeStruct((length, pairs * pair), BF)] * 3,
        scratch_shapes=[
            pltpu.VMEM((pair, length), BF),
            pltpu.VMEM((length, pair), F32),
            pltpu.VMEM((length, pair), F32),
        ],
        compiler_params=params(),
        cost_estimate=pl.CostEstimate(
            flops=20 * pairs * length * length * HEAD_DIM,
            bytes_accessed=16 * length * pairs * pair,
            transcendentals=pairs * length * length,
        ),
        name="self_backward",
    )(qkv, qkv, qkv, do, segc, segr, lse)


def stack_heads(block):
    rows = block.shape[0]
    return jnp.concatenate(
        [jnp.where(head_mask(rows, head), block, 0) for head in range(2)], 0
    ).astype(BF)


def unstack_heads(block):
    rows = block.shape[0] // 2
    return jnp.where(head_mask(rows, 0), block[:rows], block[rows:])


def cross_weights(k, qs):
    s = dot_nt(k, qs)
    e = jnp.exp(s - jnp.max(s, 0, keepdims=True))
    return e, jnp.sum(e, 0, keepdims=True)


def cross_fwd_kernel(q_ref, k_ref, v_ref, o_ref):
    pair = 2 * HEAD_DIM
    for at in range(0, q_ref.shape[1], pair):
        cols = slice(at, at + pair)
        qs = stack_heads(q_ref[:, cols] * SCALE)
        e, total = cross_weights(k_ref[:, cols], qs)
        o = dot_tn((e / total).astype(BF), v_ref[:, cols])
        o_ref[:, cols] = unstack_heads(o).astype(BF)


def cross_forward(cq, ckv):
    tokens, width = cq.shape
    spans = tokens // SPAN
    memory = ckv.shape[0] // spans
    return pl.pallas_call(
        cross_fwd_kernel,
        grid=(spans,),
        in_specs=[
            pl.BlockSpec((SPAN, width), lambda i: (i, 0)),
            pl.BlockSpec((memory, width), lambda i: (i, 0)),
            pl.BlockSpec((memory, width), lambda i: (i, 1)),
        ],
        out_specs=pl.BlockSpec((SPAN, width), lambda i: (i, 0)),
        out_shape=jax.ShapeDtypeStruct((tokens, width), BF),
        compiler_params=params(),
        cost_estimate=pl.CostEstimate(
            flops=4 * tokens * memory * width,
            bytes_accessed=4 * tokens * width + 4 * spans * memory * width,
            transcendentals=tokens * memory * HEADS,
        ),
        name="cross_forward",
    )(cq, ckv, ckv)


def cross_bwd_kernel(q_ref, k_ref, v_ref, do_ref, dq_ref, dkv_ref):
    pair = 2 * HEAD_DIM
    width = q_ref.shape[1]
    for at in range(0, width, pair):
        cols = slice(at, at + pair)
        qs = stack_heads(q_ref[:, cols] * SCALE)
        dos = stack_heads(do_ref[:, cols])
        k = k_ref[:, cols]
        e, total = cross_weights(k, qs)
        p = e / total
        dp = dot_nt(v_ref[:, cols], dos)
        delta = jnp.sum(p * dp, 0, keepdims=True)
        ds = (p * (dp - delta)).astype(BF)
        dq_ref[:, cols] = (unstack_heads(dot_tn(ds, k)) * SCALE).astype(BF)
        dkv_ref[:, cols] = dot(ds, qs).astype(BF)
        dkv_ref[:, width + at : width + at + pair] = dot(p.astype(BF), dos).astype(BF)


def cross_backward(cq, ckv, do):
    tokens, width = cq.shape
    spans = tokens // SPAN
    memory = ckv.shape[0] // spans
    return pl.pallas_call(
        cross_bwd_kernel,
        grid=(spans,),
        in_specs=[
            pl.BlockSpec((SPAN, width), lambda i: (i, 0)),
            pl.BlockSpec((memory, width), lambda i: (i, 0)),
            pl.BlockSpec((memory, width), lambda i: (i, 1)),
            pl.BlockSpec((SPAN, width), lambda i: (i, 0)),
        ],
        out_specs=[
            pl.BlockSpec((SPAN, width), lambda i: (i, 0)),
            pl.BlockSpec((memory, 2 * width), lambda i: (i, 0)),
        ],
        out_shape=[
            jax.ShapeDtypeStruct((tokens, width), BF),
            jax.ShapeDtypeStruct((spans * memory, 2 * width), BF),
        ],
        compiler_params=params(),
        cost_estimate=pl.CostEstimate(
            flops=10 * tokens * memory * width,
            bytes_accessed=6 * tokens * width + 8 * spans * memory * width,
            transcendentals=tokens * memory * HEADS,
        ),
        name="cross_backward",
    )(cq, ckv, ckv, do)


def ffn_kernel(h_ref, dy_ref, *refs, quarters, carry, chunk):
    ups, downs = refs[:quarters], refs[quarters : 2 * quarters]
    rest = refs[2 * quarters :]
    if carry:
        y0_ref, dh0_ref, rest = rest[0], rest[1], rest[2:]
    y_ref, dh_ref = rest[0], rest[1]
    grads = rest[2:]
    step = pl.program_id(0)
    width = h_ref.shape[1]

    @pl.when(step == 0)
    def _():
        y_ref[...] = y0_ref[...] if carry else jnp.zeros_like(y_ref)
        dh_ref[...] = dh0_ref[...] if carry else jnp.zeros_like(dh_ref)

    h = h_ref[...]
    dy = dy_ref[...]
    at = pl.multiple_of(step * chunk, chunk)
    for up_ref, down_ref, g_ref in zip(ups, downs, grads):
        up, down = up_ref[...], down_ref[...]
        u = dot(h, up)
        t = jnp.tanh(GELU_A * (u + GELU_B * (u * u * u)))
        gl = (0.5 * u * (1.0 + t)).astype(BF)
        y_ref[...] += dot(gl, down)
        slope = 0.5 * (1.0 + t) + 0.5 * u * (1.0 - t * t) * (GELU_A * (1.0 + 3.0 * GELU_B * (u * u)))
        du = (dot_nt(dy, down) * slope).astype(BF)
        dh_ref[...] += dot_nt(du, up)
        g_ref[:, pl.ds(at, chunk)] = dot_tn(h, du).astype(BF)
        g_ref[pl.ds(at, chunk), pl.ds(width, width)] = dot_tn(gl, dy).astype(BF)


def feed_forward(h, dy, weights, carry=None):
    tokens, width = h.shape
    n = len(weights)
    hidden = weights[0].shape[0]
    chunk = 256
    whole = pl.BlockSpec((tokens, width), lambda j: (0, 0))
    operands = [h, dy, *weights, *weights]
    in_specs = [whole, whole]
    in_specs += [pl.BlockSpec((width, chunk), lambda j: (0, j))] * n
    in_specs += [pl.BlockSpec((chunk, width), lambda j: (j, 1))] * n
    if carry is not None:
        operands += list(carry)
        in_specs += [whole, whole]
    out = pl.pallas_call(
        functools.partial(ffn_kernel, quarters=n, carry=carry is not None, chunk=chunk),
        grid=(hidden // chunk,),
        in_specs=in_specs,
        out_specs=[whole, whole] + [pl.BlockSpec((hidden, 2 * width), lambda j: (0, 0))] * n,
        out_shape=[jax.ShapeDtypeStruct((tokens, width), F32)] * 2
        + [jax.ShapeDtypeStruct((hidden, 2 * width), BF)] * n,
        compiler_params=params(),
        cost_estimate=pl.CostEstimate(
            flops=12 * n * tokens * width * hidden,
            bytes_accessed=8 * n * width * hidden + 16 * tokens * width,
            transcendentals=n * tokens * hidden,
        ),
        name="feed_forward",
    )(*operands)
    return out[0], out[1], out[2:]


def assemble_kernel(idx_ref, *refs, counts, rows):
    pieces, out_ref, sem = refs[: len(counts)], refs[len(counts)], refs[len(counts) + 1]
    copies = []
    for piece, count in zip(pieces, counts):
        for j in range(count):
            i = len(copies)
            at = pl.multiple_of(idx_ref[i] * rows, rows)
            copies.append(
                pltpu.make_async_copy(
                    piece.at[pl.ds(j * rows, rows), :], out_ref.at[pl.ds(at, rows), :], sem.at[i]
                )
            )
    for copy in copies:
        copy.start()
    for copy in copies:
        copy.wait()


def assemble(pieces, places, rows):
    counts = [p.shape[0] // rows for p in pieces]
    cols, n = pieces[0].shape[1], sum(counts)
    return pl.pallas_call(
        functools.partial(assemble_kernel, counts=counts, rows=rows),
        grid_spec=pltpu.PrefetchScalarGridSpec(
            num_scalar_prefetch=1,
            grid=(1,),
            in_specs=[pl.BlockSpec(memory_space=pl.ANY)] * len(pieces),
            out_specs=pl.BlockSpec((n * rows, cols), lambda i, idx: (0, 0)),
            scratch_shapes=[pltpu.SemaphoreType.DMA((n,))],
        ),
        out_shape=jax.ShapeDtypeStruct((n * rows, cols), pieces[0].dtype),
        compiler_params=params(),
        cost_estimate=pl.CostEstimate(
            flops=0, bytes_accessed=4 * n * rows * cols, transcendentals=0
        ),
        name="assemble",
    )(jnp.stack(places).astype(jnp.int32), *pieces)


def merge_kernel(c_ref, own_ref, far_ref, *refs, sizes):
    outs, sem = refs[:-1], refs[-1]
    copies, start = [], 0
    for out_ref, size in zip(outs, sizes):
        for source, side in ((own_ref, c_ref[0]), (far_ref, 1 - c_ref[0])):
            at = pl.multiple_of(side * size, size)
            copies.append(
                pltpu.make_async_copy(
                    source.at[:, pl.ds(start, size)], out_ref.at[:, pl.ds(at, size)], sem.at[len(copies)]
                )
            )
        start += size
    for copy in copies:
        copy.start()
    for copy in copies:
        copy.wait()


def merge(own, far, c, sizes):
    rows = own.shape[0]
    return pl.pallas_call(
        functools.partial(merge_kernel, sizes=sizes),
        grid_spec=pltpu.PrefetchScalarGridSpec(
            num_scalar_prefetch=1,
            grid=(1,),
            in_specs=[pl.BlockSpec(memory_space=pl.ANY)] * 2,
            out_specs=[pl.BlockSpec((rows, 2 * n), lambda i, idx: (0, 0)) for n in sizes],
            scratch_shapes=[pltpu.SemaphoreType.DMA((2 * len(sizes),))],
        ),
        out_shape=[jax.ShapeDtypeStruct((rows, 2 * n), own.dtype) for n in sizes],
        compiler_params=params(),
        cost_estimate=pl.CostEstimate(
            flops=0, bytes_accessed=8 * rows * sum(sizes), transcendentals=0
        ),
        name="merge",
    )(c.reshape(1).astype(jnp.int32), own, far)


def join_kernel(c_ref, own_ref, far_ref, *outs, layout, size):
    start = 0
    for out_ref, segments, width in layout_refs(outs, layout):
        for j in range(segments):
            for source, side in ((own_ref, c_ref[0]), (far_ref, 1 - c_ref[0])):
                at = pl.multiple_of(side * width, size)
                out_ref[:, pl.ds(at + 2 * j * width, width)] = source[:, start : start + width].astype(F32)
            start += width


def layout_refs(outs, layout):
    return [(o, n, w) for o, (n, w) in zip(outs, layout)]


def join(own, far, c, layout):
    rows = own.shape[0]
    shapes = [jax.ShapeDtypeStruct((rows, 2 * n * w), F32) for n, w in layout]
    return pl.pallas_call(
        functools.partial(join_kernel, layout=layout, size=128),
        grid_spec=pltpu.PrefetchScalarGridSpec(
            num_scalar_prefetch=1,
            grid=(1,),
            in_specs=[pl.BlockSpec(v.shape, lambda i, idx: (0, 0)) for v in (own, far)],
            out_specs=[pl.BlockSpec(v.shape, lambda i, idx: (0, 0)) for v in shapes],
        ),
        out_shape=shapes,
        compiler_params=params(),
        name="join",
    )(c.reshape(1).astype(jnp.int32), own, far)


def spread_kernel(p_ref, up_ref, down_ref, *, unit):
    quarters, rows, cols = p_ref.shape
    width = cols // 2
    for s in range(quarters):
        for f in range(width // unit):
            up_ref[:, (f * quarters + s) * unit : (f * quarters + s + 1) * unit] = p_ref[
                s, :, f * unit : (f + 1) * unit
            ].astype(F32)
        down_ref[s * rows : (s + 1) * rows, :] = p_ref[s, :, width:].astype(F32)


def spread(pieces, unit):
    quarters, rows, cols = pieces.shape
    return pl.pallas_call(
        functools.partial(spread_kernel, unit=unit),
        out_shape=[
            jax.ShapeDtypeStruct((rows, quarters * cols // 2), F32),
            jax.ShapeDtypeStruct((quarters * rows, cols // 2), F32),
        ],
        compiler_params=params(),
        name="spread",
    )(pieces)


def grad_kernel(side_ref, a_ref, b_ref, *refs):
    out_ref = refs[-1]
    total = dot_tn(a_ref[...], b_ref[...])
    if len(refs) == 2:
        total = total + refs[0][...].astype(F32)
    out_ref[...] = total.astype(BF)


def grad_half(a, b, side, more=None):
    tokens, rows = a.shape
    cols = b.shape[1] // 2
    block = 384
    blocks = cols // block
    operands = [a, b] + ([] if more is None else [more])
    out_spec = pl.BlockSpec((rows, block), lambda j, side: (0, j))
    return pl.pallas_call(
        grad_kernel,
        grid_spec=pltpu.PrefetchScalarGridSpec(
            num_scalar_prefetch=1,
            grid=(blocks,),
            in_specs=[
                pl.BlockSpec((tokens, rows), lambda j, side: (0, 0)),
                pl.BlockSpec((tokens, block), lambda j, side: (0, side[0] * blocks + j)),
            ]
            + [out_spec] * (len(operands) - 2),
            out_specs=out_spec,
        ),
        out_shape=jax.ShapeDtypeStruct((rows, cols), BF),
        compiler_params=params(),
        cost_estimate=pl.CostEstimate(
            flops=2 * tokens * rows * cols,
            bytes_accessed=2 * tokens * (rows + cols) + 4 * rows * cols,
            transcendentals=0,
        ),
        name="grad_half",
    )(side.reshape(1).astype(jnp.int32), *operands)


class Place:
    def __init__(self):
        self.n = lax.axis_size("fsdp")
        f = lax.axis_index("fsdp")
        s = lax.axis_index("seq")
        self.z, self.y = f // 2, f % 2
        self.x, self.c = s // 2, s % 2
        self.s = s
        self.direct = self.n == 8

    def swap_core(self, value):
        return lax.ppermute(value, "seq", [(0, 1), (1, 0), (2, 3), (3, 2)])

    def swap_x(self, value):
        return lax.ppermute(value, "seq", [(0, 2), (2, 0), (1, 3), (3, 1)])

    def swap_y(self, value):
        return lax.ppermute(value, "fsdp", [(i, i ^ 1) for i in range(self.n)])

    def shift_z(self, value, hops):
        return lax.ppermute(value, "fsdp", [(i, (i + 2 * hops) % self.n) for i in range(self.n)])

    def places(self):
        base = [2 * ((self.z - k) % 4) for k in range(4)]
        return [b + self.y for b in base] + [b + 1 - self.y for b in base]

    def shifts(self, piece):
        return [self.shift_z(piece, k) for k in (1, 2, 3)]

    def send_y(self, mats):
        mats = [m.reshape(self.n // 2, 2, -1, m.shape[1]) for m in mats]
        sent = jnp.concatenate([pick(m, 1 - self.y, 1).astype(BF) for m in mats], 2)
        kept = jnp.concatenate([pick(m, self.y, 1).astype(BF) for m in mats], 2)
        return sent, kept

    def send_z(self, column):
        own = pick(column, self.z, 0)
        if not self.direct:
            total = lax.psum(column, "fsdp")
            return own, [pick(total, self.z, 0)]
        return own, [self.shift_z(pick(column, (self.z + k) % 4, 0), k) for k in (1, 2, 3)]

    def total(self, own, got):
        if not self.direct:
            return got[0].astype(F32)
        return sum((g.astype(F32) for g in got), own.astype(F32))


def tie(*values):
    return lax.optimization_barrier(values)


def added(first, second):
    return (first.astype(F32) + second.astype(F32)).astype(BF)


def pick(value, index, axis):
    return lax.dynamic_index_in_dim(value, index, axis, keepdims=False)


def ordered(flag, first, second, axis):
    low = jnp.where(flag == 0, first, second)
    high = jnp.where(flag == 0, second, first)
    return jnp.stack([low, high], axis)


def norm_stats(values):
    centre = values - jnp.mean(values, -1, keepdims=True)
    r = lax.rsqrt(jnp.mean(centre * centre, -1, keepdims=True) + EPS)
    return centre * r, r


def norm(values, gain, bias):
    xhat, _ = norm_stats(values)
    return (xhat * gain + bias).astype(BF)


def norm_back(values, gain, dh):
    xhat, r = norm_stats(values)
    dg = dh * gain
    dv = r * (
        dg - jnp.mean(dg, -1, keepdims=True) - xhat * jnp.mean(dg * xhat, -1, keepdims=True)
    )
    return dv, jnp.sum(dh * xhat, 0), jnp.sum(dh, 0)


def per_device(
    inputs, segments, neighbours,
    ln1_gain, ln1_bias, w_qkv, w_attn_out, ln2_gain, ln2_bias, cross_q, cross_kv, cross_out,
    ln3_gain, ln3_bias, w_up, w_down, out_grad,
):
    at = Place()
    x, c = at.x, at.c
    seqs, piece, width = inputs.shape
    half = width // 2
    rows = w_qkv.shape[0]
    tokens = seqs * piece

    theirs = at.swap_x(pick(inputs, 1 - x, 0))
    mine = pick(inputs, x, 0)
    blocks = ordered(x, mine, theirs, 0)
    sequence = ordered(c, blocks, at.swap_core(blocks), 1).reshape(4 * piece, width)
    seg = pick(segments, x, 0)
    segc, segr = seg[:, None], seg[None, :]

    vectors = jnp.stack([ln1_gain, ln1_bias, ln2_gain, ln2_bias, ln3_gain, ln3_bias], 1)
    vectors = jnp.pad(vectors, ((0, 0), (0, 128 - vectors.shape[1])))
    piece_a = jnp.concatenate(
        [lax.dynamic_slice_in_dim(w_qkv, j * width + c * half, half, 1) for j in range(3)] + [vectors], 1
    )

    def half_of(weight):
        return lax.dynamic_slice_in_dim(weight, c * (weight.shape[1] // 2), weight.shape[1] // 2, 1)

    piece_b = jnp.concatenate([half_of(w) for w in (cross_kv, w_attn_out, cross_q, cross_out)], 1)
    unit = w_down.shape[0] // 4
    up_quarter = pick(w_up.reshape(rows, -1, 4, unit), at.s, 2).reshape(rows, -1)
    down_quarter = pick(w_down.reshape(4, unit, width), at.s, 0)
    piece_f = jnp.concatenate([up_quarter, down_quarter], 1)
    if at.direct:
        places = at.places()
        first = at.swap_y(piece_a)
        zs, first, piece_f = tie(at.shifts(piece_a), first, piece_f)
        others = at.swap_y(jnp.concatenate(zs, 0))
        zs_f, others, piece_b = tie(at.shifts(piece_f), others, piece_b)
        group_a = assemble([piece_a, *zs, first, others], places, rows)
        column_f = jnp.concatenate([piece_f, *zs_f], 0)
        moving = (at.swap_x(column_f), at.swap_y(column_f), at.shifts(piece_b))
    else:
        group_a = lax.all_gather(piece_a, "fsdp", axis=0, tiled=True)
        moving = ()
    wqkv = group_a[:, : 3 * half]
    gains = group_a[:, 3 * half : 3 * half + 6].T.astype(F32)
    g1, b1, g2, b2, g3, b3 = (gains[i] for i in range(6))

    seqf = sequence.astype(F32)
    h1 = norm(seqf, g1, b1)
    qkv = dot(h1, wqkv).astype(BF)
    qkv, moving = tie(qkv, moving)
    if at.direct:
        xcolumn, others_f, zs_b = moving
        column_b = jnp.concatenate([piece_b, *zs_b], 0)
        moving = (at.swap_x(others_f), at.swap_y(column_b))
    att_heads, lse = self_forward(qkv, segc, segr)
    by_x = att_heads.reshape(2, 2, piece, half)
    got = at.swap_x(pick(by_x, 1 - x, 0))
    chip, moving = tie(ordered(x, pick(by_x, x, 0), got, 0), moving)
    got = at.swap_core(pick(chip, 1 - c, 1))
    att = ordered(c, pick(chip, c, 1), got, 2).reshape(tokens, width)
    if at.direct:
        group_b = assemble([column_b, moving[1]], places, rows)
        q00 = assemble([column_f, others_f], places, rows)
        q10 = assemble([xcolumn, moving[0]], places, rows)
    else:
        group_b = lax.all_gather(piece_b, "fsdp", axis=0, tiled=True)
        q00 = lax.all_gather(piece_f, "fsdp", axis=0, tiled=True)
        q10 = at.swap_x(q00)
    wckv, wao, wcq, wco = merge(group_b, at.swap_core(group_b), c, (width, half, half, half))
    q01 = at.swap_core(q00)
    q11 = at.swap_core(q10)

    xin = inputs.reshape(tokens, width).astype(F32)
    x1 = xin + dot(att, wao)
    h2 = norm(x1, g2, b2)
    cq = dot(h2, wcq).astype(BF)
    nb = neighbours.reshape(-1, width)
    ckv = dot(nb, wckv).astype(BF)
    cro = cross_forward(cq, ckv)
    x2 = x1 + dot(cro, wco)
    h3 = norm(x2, g3, b3)
    dy = out_grad.reshape(tokens, width)
    y, dh3, far_grads = feed_forward(h3, dy, [q01, q11])
    f0 = at.swap_core(far_grads[0])
    f1 = at.swap_core(far_grads[1])
    y, dh3, own_grads = feed_forward(h3, dy, [q00, q10], (y, dh3))
    outputs = (x2 + y).astype(BF).reshape(seqs, piece, width)

    away, dh3 = tie(added(own_grads[1], f1), dh3)
    ffn_got = at.swap_x(away)

    dv3, gg3, gb3 = norm_back(x2, g3, dh3)
    dx2 = dy.astype(F32) + dv3
    dc = dx2.astype(BF)
    dcro = dot_nt(dc, wco).astype(BF)
    dcq, dckv = cross_backward(cq, ckv, dcro)
    dh2 = dot_nt(dcq, wcq)
    dv2, gg2, gb2 = norm_back(x1, g2, dh2)
    dx1 = dx2 + dv2
    da = dx1.astype(BF)
    datt = dot_nt(da, wao).astype(BF)
    pairs = ((nb, dckv), (att, da), (h2, dcq), (cro, dc))
    sent_b = [grad_half(a, b, 1 - c) for a, b in pairs]
    datt, sent_b, ffn_got = tie(datt, sent_b, ffn_got)
    ffn_sum = own_grads[0].astype(F32) + f0.astype(F32) + ffn_got.astype(F32)
    ffn_own = lax.psum_scatter(
        ffn_sum.astype(BF).reshape(at.n, rows, 2 * width), "fsdp", scatter_dimension=0, tiled=False
    )
    sums_b = [grad_half(a, b, c, at.swap_core(v)) for (a, b), v in zip(pairs, sent_b)]
    sent_b, kept_b = at.send_y(sums_b)
    neighbour_grad = dot_nt(dckv, wckv)

    datt = datt.reshape(seqs, piece, 2, half)
    got = at.swap_core(pick(datt, 1 - c, 2))
    chip = ordered(c, pick(datt, c, 2), got, 1)
    got = at.swap_x(pick(chip, 1 - x, 0))
    do = ordered(x, pick(chip, x, 0), got, 0).reshape(4 * piece, half)
    do, sent_b = tie(do, sent_b)
    got_b = at.swap_y(sent_b)
    dqkv = jnp.concatenate(self_backward(qkv, do, segc, segr, lse), 1)
    dqkv, got_b = tie(dqkv, got_b)
    moving_b = at.send_z(added(kept_b, got_b))
    grad_qkv = dot_tn(h1, dqkv).astype(BF)
    sent_a, kept_a = at.send_y([grad_qkv])
    part = dot_nt(dqkv, wqkv).astype(BF).reshape(2, 2, piece, width)
    part, sent_a = tie(part, sent_a)
    got_a = at.swap_y(sent_a)
    got = at.swap_core(pick(part, 1 - c, 1))
    chip = (pick(part, c, 1).astype(F32) + got.astype(F32)).astype(BF)
    got = at.swap_x(pick(chip, 1 - x, 0))
    dh1 = ordered(x, pick(chip, x, 0), got, 0).reshape(tokens, width).astype(F32)
    dv1, gg1, gb1 = norm_back(xin, g1, dh1)
    input_grad = (dx1 + dv1).reshape(seqs, piece, width)

    def finish(own):
        return own + at.swap_x(own.astype(BF)).astype(F32)

    input_grad, moving_b, got_a = tie(input_grad, moving_b, got_a)
    vec = jnp.stack([gg1, gb1, gg2, gb2, gg3, gb3], 0)
    vec = vec + at.swap_core(vec)
    vec = jnp.pad((vec + at.swap_y(vec)).T, ((0, 0), (0, 128 - 6)))
    vec = pick(vec.reshape(at.n // 2, 2, rows, 128), at.y, 1).astype(BF)
    moving_a = at.send_z(jnp.concatenate([added(kept_a, got_a), vec], 2))
    ffn_x = ordered(x, ffn_own, at.swap_x(ffn_own), 0)
    ffn_all = ordered(c, ffn_x, at.swap_core(ffn_x), 1).reshape(4, rows, 2 * width)
    grad_up, grad_down = spread(ffn_all, unit)
    own_b = finish(at.total(*moving_b))
    far_b = at.swap_core(own_b.astype(BF))
    out_ckv, out_ao, out_cq, out_co = join(
        own_b, far_b, c, ((1, width), (1, half), (1, half), (1, half))
    )
    own_a = finish(at.total(*moving_a))
    far_a = at.swap_core(own_a[:, : 3 * half].astype(BF))
    (out_qkv,) = join(own_a, far_a, c, ((3, half),))
    vecs = own_a[:, 3 * half : 3 * half + 6].T

    return (
        outputs, input_grad, neighbour_grad.reshape(neighbours.shape),
        vecs[0], vecs[1], out_qkv, out_ao, vecs[2], vecs[3], out_cq, out_ckv, out_co,
        vecs[4], vecs[5], grad_up, grad_down,
    )


def solution(mesh):
    row, mat = P("fsdp"), P("fsdp", None)
    tok, mem = P("fsdp", "seq", None), P("fsdp", "seq", None, None)
    weights = (row, row, mat, mat, row, row, mat, mat, mat, row, row, mat, mat)
    return jax.shard_map(
        per_device,
        mesh=mesh,
        in_specs=(tok, mat, mem, *weights, tok),
        out_specs=(tok, tok, mem, *weights),
        check_vma=False,
    )
```
